128 devices in a mesh: patch: 8 (over z, core), mode: 16 (over x, y).
Axes of the slice: x: 4, y: 4, z: 4, core: 2. Of those that a mesh axis runs over, the one named last changes fastest.
Arguments:
- sky_map: bfloat16 [64, 8192, 64], P('patch', 'mode'), may hold values from -6 to 6
- pixel_mask: int32 [64, 8192], P('patch', 'mode'), may hold values 0 or 1
- noise_factor: float32 [64, 16, 64, 64], P('patch', 'mode'), as said below
- cycle_legendre: float32 [64, 6144, 8], P('patch', 'mode'), may hold values from -6 to 6
- band_power: float32 [6144, 8], P('mode', 'patch'), may hold values from 0.1 to 10
- channel_cov: float32 [64, 64], replicated
- test_matrix: bfloat16 [8, 6144, 2, 512], P('patch', 'mode'), may hold values from -6 to 6
Outputs:
- sketch: float32 [64, 512], P(None, ('patch', 'mode'))
The draws below stay inside these ranges and needn't reach their ends.
Inputs may be any that keep to these rules, and one draw needn't show every extreme that they name: `noise_factor`: each noise factor is lower triangular with a positive diagonal.
All inputs are finite; a program needn't handle non-finite values. No bound on the sum of `pixel_mask` on one device may be relied on, other than what follows from the above.
Results may differ from the reference program's by a relative error of at most 0.017.
Values may be sent and summed in bfloat16 or wider, within the bound.
A program may use at most 64 MiB of HBM per device.

```python
import math
import jax
import jax.numpy as jnp
from jax import lax

C = 64
NPHI = 8192
MMAX = 6144
NS = 512
CYCLES = 64
LW = 8
PIECES = 16
NPHI_DEV = 512


def draw_noise_factor(key, part):
    first, second = jax.random.split(key, 2)
    spread = jax.random.uniform(first, (CYCLES, PIECES, C, C), jnp.float32, -1.0, 1.0) / math.sqrt(C)
    lower = jnp.tril(spread, -1)
    diag = jnp.exp(jax.random.uniform(second, (CYCLES, PIECES, C), jnp.float32, math.log(0.5), math.log(2.0)))
    return lower + diag[:, :, :, None] * jnp.eye(C, dtype=jnp.float32)


def draw_channel_cov(key, part):
    first, second = jax.random.split(key, 2)
    spread = jax.random.uniform(first, (C, C), jnp.float32, -1.0, 1.0) / math.sqrt(C)
    symmetric = 0.5 * (spread + jnp.transpose(spread))
    diag = jnp.exp(jax.random.uniform(second, (C,), jnp.float32, 0.0, math.log(4.0)))
    return symmetric + diag[:, None] * jnp.eye(C, dtype=jnp.float32)


def with_ends(values, own_key, smallest, high):
    shape = values.shape
    spot = [jax.random.randint(jax.random.fold_in(own_key, axis), (), 0, shape[axis]) for axis in range(len(shape))]
    values = values.at[tuple(spot)].set(smallest)
    longest = shape.index(max(shape))
    spot[longest] = (spot[longest] + 1) % shape[longest]
    return values.at[tuple(spot)].set(high)


def spiked(drawn, rng, source, target, shards_of, factor):
    owner, partner = [(jnp.arange(drawn.shape[position]) // (drawn.shape[position] // shards_of)).reshape([-1 if axis == position else 1 for axis in range(drawn.ndim)]) for position in (source, target)]
    chosen = jax.random.permutation(rng, shards_of)[partner]
    strong = (owner == chosen) | (owner == (partner + shards_of // 2) % shards_of)
    return jnp.where(strong, factor * drawn, drawn)


def block_levels(rng, dims, cuts, low, top_value):
    level, own = 1.0, jax.random.fold_in(rng, 6)
    for position, parts in cuts:
        heights = jnp.exp(jax.random.uniform(jax.random.fold_in(own, position), (parts,), jnp.float32, low / len(cuts), top_value / len(cuts)))
        level = level * jnp.repeat(heights, dims[position] // parts).reshape([-1 if axis == position else 1 for axis in range(len(dims))])
    return level


def scatter_about(key, shape, width, limit, shards=(), kind=jnp.bfloat16):
    array = jax.random.normal(key, shape, jnp.float32) * width
    if len(shards) > 0:
        array = block_levels(key, shape, shards, -0.22, 0.18) * array
    return jnp.clip(array, min=-limit, max=limit).astype(kind)


def noise_with(own_key, dims, deviation, limit, cuts, heavy, kind=jnp.bfloat16):
    array = deviation * jax.random.normal(own_key, dims, jnp.float32)
    if cuts:
        array = array * block_levels(own_key, dims, cuts, -0.22, 0.18)
    return jnp.clip(spiked(array, jax.random.fold_in(own_key, 3), *heavy), -limit, limit).astype(kind)


def setup_inputs(seed: int = 0) -> dict:
    keys = jax.random.split(jax.random.key(seed), 8)
    return {
        "sky_map": scatter_about(keys[0], (CYCLES, NPHI, C), 1.0, 6.0, ((0, 8), (1, 16))),
        "pixel_mask": with_ends((jax.random.randint(keys[1], (CYCLES, NPHI), 0, 4) < 3).astype(jnp.int32), jax.random.fold_in(keys[1], 1), 0, 1),
        "noise_factor": draw_noise_factor(jax.random.fold_in(keys[7], 71), 0),
        "cycle_legendre": scatter_about(keys[3], (CYCLES, MMAX, LW), 1.0, 6.0, ((0, 8), (1, 16)), jnp.float32),
        "band_power": jnp.clip(jnp.exp(math.log(10.0) - 4.6051702 * jax.random.uniform(keys[4], (MMAX, LW), jnp.float32) ** block_levels(keys[4], (MMAX, LW), ((0, 16), (1, 8)), -0.2, 0.2)), 0.1, 10.0),
        "channel_cov": draw_channel_cov(jax.random.fold_in(keys[7], 71), 0),
        "test_matrix": noise_with(keys[6], (LW, MMAX, 2, NS), 1.0, 6.0, ((0, 8), (1, 16)), (1, 3, 16, 2.0)),
    }


def reference(sky_map, pixel_mask, noise_factor, cycle_legendre, band_power, channel_cov, test_matrix):
    pieces = sky_map.astype(jnp.float32).reshape(CYCLES, PIECES, NPHI_DEV, C)
    white = jnp.einsum("rqdc,rqjc->rqjd", noise_factor, pieces, precision=lax.Precision.HIGHEST)
    white = white.reshape(CYCLES, NPHI, C) * pixel_mask.astype(jnp.float32)[:, :, None]
    whitened = white.astype(jnp.bfloat16).astype(jnp.float32)
    spectrum = jnp.fft.fft(whitened, axis=1)[:, :MMAX]
    four = jnp.stack([jnp.real(spectrum), jnp.imag(spectrum)], axis=2).astype(jnp.float32)
    alm = jnp.einsum("rmk,rmtc->kmtc", cycle_legendre, four, precision=lax.Precision.HIGHEST)
    mixed = jnp.einsum("dc,kmtc->kmtd", channel_cov, alm, precision=lax.Precision.HIGHEST)
    scaled = (mixed * jnp.transpose(band_power)[:, :, None, None]).astype(jnp.bfloat16)
    left = scaled.reshape(LW * MMAX * 2, C)
    right = test_matrix.reshape(LW * MMAX * 2, NS)
    return jnp.dot(jnp.transpose(left), right, preferred_element_type=jnp.float32)
```

```python
import functools
import math

import jax
import jax.numpy as jnp
import numpy as np
from jax import lax
from jax.experimental import pallas as pl
from jax.experimental.pallas import tpu as pltpu
from jax.sharding import PartitionSpec as P

F32 = jnp.float32
BF16 = jnp.bfloat16
MESH = pl.DeviceIdType.MESH
NM = 16
NP = 8


def fourier_tables():
    m1 = np.arange(64)[:, None]
    j1 = np.arange(64)[None, :]
    angle = 2.0 * math.pi * ((m1 * j1) % 64) / 64.0
    wa = np.concatenate([np.cos(angle), -np.sin(angle)], axis=0)
    low = np.arange(128)[:, None]
    j2 = np.arange(128)[None, :]
    turn = 2.0 * math.pi * (low * j2) / 8192.0
    wb = np.zeros((48, 2, 4, 4, 2, 64))
    g = np.arange(48)[:, None]
    fold = np.arange(64)[None, :]
    phi = 2.0 * math.pi * ((g * fold) % 64) / 64.0
    for dd in range(4):
        wb[:, 0, dd, dd, 0, :] = np.cos(phi)
        wb[:, 0, dd, dd, 1, :] = np.sin(phi)
        wb[:, 1, dd, dd, 0, :] = -np.sin(phi)
        wb[:, 1, dd, dd, 1, :] = np.cos(phi)
    return (
        jnp.asarray(wa.astype(np.float32), BF16),
        jnp.asarray(wb.reshape(384, 512).astype(np.float32), BF16),
        jnp.asarray(np.cos(turn), F32),
        jnp.asarray(np.sin(turn), F32),
    )


def iota2(shape, axis):
    return lax.broadcasted_iota(jnp.int32, shape, axis)


def onehot(test):
    return jnp.where(test, 1.0, 0.0).astype(BF16)


def dot(a, b):
    return jnp.dot(a, b, preferred_element_type=F32)


def dot_nt(a, b):
    return lax.dot_general(a, b, (((1,), (1,)), ((), ())), preferred_element_type=F32)


def kernel(
    sky_h, mask_h, noise_h, leg_h, band_h, cov_h, test_h, wa_h, wb_h, twc_h, tws_h,
    out,
    sky, mask, noise, leg, band, cov, test, wa, wb, twc, tws,
    bd, xsend, xrecv, xs, lown, lall, lf, four, alm_a, alm_b, pair, zsend, zrecv,
    total, asend, arecv, tt, ce, fsend, frecv, gsend, grecv,
    in_sem, xs_sem, xr_sem, ls_sem, lr_sem, ps_sem, pr_sem, zs_sem, zr_sem,
    as_sem, ar_sem, fs_sem, fr_sem, gs_sem, gr_sem,
):
    p = lax.axis_index("patch")
    e = lax.axis_index("mode")
    core = lax.rem(p, 2)
    z = p // 2

    barrier = pltpu.get_barrier_semaphore()
    for i in range(1, NM):
        pl.semaphore_signal(barrier, inc=1, device_id=(p, lax.rem(e + i, NM)), device_id_type=MESH)
    for i in range(1, NP):
        pl.semaphore_signal(barrier, inc=1, device_id=(lax.rem(p + i, NP), e), device_id_type=MESH)

    hbm = (noise_h, sky_h, mask_h, leg_h, wa_h, twc_h, tws_h, wb_h, cov_h, band_h, test_h)
    vmem = (noise, sky, mask, leg, wa, twc, tws, wb, cov, band, test)
    loads = [pltpu.make_async_copy(a, b, in_sem.at[i]) for i, (a, b) in enumerate(zip(hbm, vmem))]
    for load in loads:
        load.start()

    row = iota2((512, 512), 0)
    lane = iota2((512, 512), 1)
    source = ((row >> 2) & 7) * 64 + (row >> 5) * 4 + (row & 3)
    order = onehot(lane == source)
    repeat = onehot((iota2((64, 512), 1) & 63) == iota2((64, 512), 0))
    loads[0].wait()
    moved = dot(order, noise[...].astype(BF16)).astype(BF16)
    wide = dot(moved, repeat)
    bd[...] = jnp.where((lane >> 6) == ((row >> 2) & 7), wide, 0.0).astype(BF16)
    loads[1].wait()
    loads[2].wait()
    for r in range(8):
        seen = jnp.broadcast_to(mask[r : r + 1, :].astype(F32), (64, 512)).astype(BF16)
        sky[64 * r : 64 * r + 64, :] = sky[64 * r : 64 * r + 64, :] * seen

    loads[3].wait()
    for t in range(3):
        lown[t] = leg[:, 128 * t : 128 * t + 128].astype(BF16)

    def send_x(i):
        to = lax.rem(e + i, NM)
        return pltpu.make_async_remote_copy(
            src_ref=xsend.at[to], dst_ref=xrecv.at[e], send_sem=xs_sem.at[i], recv_sem=xr_sem.at[e],
            device_id=(p, to), device_id_type=MESH)

    def send_l(i):
        to = lax.rem(e + i, NM)
        return pltpu.make_async_remote_copy(
            src_ref=lown, dst_ref=lall.at[e], send_sem=ls_sem.at[i], recv_sem=lr_sem.at[e],
            device_id=(p, to), device_id_type=MESH)

    for q in range(4):
        white = dot(bd[128 * q : 128 * q + 128, :], sky[...]).astype(BF16)
        xsend[4 * q : 4 * q + 4] = white.reshape(4, 32, 512)

    pl.semaphore_wait(barrier, NM - 1 + NP - 1)
    for i in range(1, NM):
        send_x(i).start()
    for i in range(1, NM):
        send_l(i).start()

    loads[10].wait()
    loads[8].wait()
    split = onehot(iota2((256, 256), 1) == 2 * (iota2((256, 256), 0) & 127) + (iota2((256, 256), 0) >> 7))
    s_to = iota2((512, 512), 1)
    s_from = ((s_to >> 2) & 7) * 64 + (s_to >> 5) * 4 + (s_to & 3)
    columns = onehot(iota2((512, 512), 0) == s_from)
    for b in range(3):
        block = test[128 * b : 128 * b + 128].reshape(256, 512)
        parts = dot(dot(split, block).astype(BF16), columns).astype(BF16)
        tt[128 * b : 128 * b + 128, :] = parts[:128]
        tt[384 + 128 * b : 384 + 128 * b + 128, :] = parts[128:]
    l128 = iota2((64, 128), 1)
    spread = onehot(iota2((64, 128), 0) == 4 * (l128 >> 3) + (l128 & 3))
    high = cov[...].astype(BF16)
    rest = (cov[...] - high.astype(F32)).astype(BF16)
    for n, piece in enumerate((high, rest)):
        wide_cov = dot(piece, spread)
        for t in range(2):
            ce[n, 64 * t : 64 * t + 64, :] = jnp.where(((l128 >> 2) & 1) == t, wide_cov, 0.0).astype(BF16)

    xrecv[e] = xsend[e]
    lall[e] = lown[...]

    def wait_x(src):
        pltpu.make_async_remote_copy(
            src_ref=xrecv.at[src], dst_ref=xrecv.at[src], send_sem=xs_sem.at[0], recv_sem=xr_sem.at[src],
            device_id=(p, e), device_id_type=MESH).wait_recv()

    def wait_l(src):
        pltpu.make_async_remote_copy(
            src_ref=lall.at[src], dst_ref=lall.at[src], send_sem=ls_sem.at[0], recv_sem=lr_sem.at[src],
            device_id=(p, e), device_id_type=MESH).wait_recv()

    def spread_x(src):
        for h in range(4):
            xs[pl.ds(src * 4 + h, 32, stride=64), :] = xrecv[src, :, 128 * h : 128 * h + 128].astype(F32)

    def spread_l(src):
        lf[pl.ds(pl.multiple_of(src * 192, 64), 192), :] = lall[src].reshape(192, 128).astype(F32)

    spread_x(e)
    spread_l(e)

    def take_x(i, carry):
        src = lax.rem(e + NM - i, NM)
        wait_x(src)
        spread_x(src)
        return carry

    lax.fori_loop(1, NM, take_x, 0)

    loads[4].wait()
    loads[5].wait()
    loads[6].wait()
    loads[7].wait()
    left_half = iota2((64, 128), 1) < 64

    def transform(pair_index, carry):
        rows = []
        for s in range(2):
            base = pair_index * 512 + s * 256
            pix = [xs[pl.ds(pl.multiple_of(base + 64 * dd, 64), 64), :] for dd in range(4)]
            first = dot(wa[...], jnp.concatenate(pix, axis=1).astype(BF16))
            lanes = []
            for dd in range(4):
                re = first[:64, 128 * dd : 128 * dd + 128]
                im = first[64:, 128 * dd : 128 * dd + 128]
                halves = []
                for h in range(2):
                    c = twc[64 * h : 64 * h + 64, :]
                    sn = tws[64 * h : 64 * h + 64, :]
                    tr = re * c + im * sn
                    ti = im * c - re * sn
                    halves.append(
                        jnp.where(left_half, tr, ti) + pltpu.roll(jnp.where(left_half, ti, tr), 64, 1))
                lanes.append(jnp.concatenate(halves, axis=0).astype(BF16))
            rows.append(jnp.concatenate(lanes, axis=1))
        second = dot_nt(wb[...], jnp.concatenate(rows, axis=0))
        four[2 * pair_index] = second[:, :128]
        four[2 * pair_index + 1] = second[:, 128:]
        return carry

    lax.fori_loop(0, 4, transform, 0)

    def take_l(i, carry):
        src = lax.rem(e + NM - i, NM)
        wait_l(src)
        spread_l(src)
        return carry

    lax.fori_loop(1, NM, take_l, 0)

    def legendre(parity, put):
        def body(gp, carry):
            acc = [[None, None] for _ in range(4)]
            for gi in range(2):
                g = 2 * gp + gi
                for r in range(8):
                    f = four[r, pl.ds(pl.multiple_of(g * 8, 8), 8), :]
                    for kk in range(4):
                        lrow = lf[pl.ds(g * 64 + r * 8 + 2 * kk + parity, 8, stride=0), :]
                        term = lrow * f
                        acc[kk][gi] = term if r == 0 else acc[kk][gi] + term
            for kk in range(4):
                put(kk, pl.ds(pl.multiple_of(gp * 16, 16), 16), jnp.concatenate(acc[kk], axis=0))
            return carry

        lax.fori_loop(0, 24, body, 0)

    def put_a(kk, rows, value):
        alm_a[kk, rows, :] = value.astype(BF16)

    def put_b(kk, rows, value):
        alm_b[kk, rows, :] = value

    legendre(1 - core, put_a)
    to_core = pltpu.make_async_remote_copy(
        src_ref=alm_a, dst_ref=pair, send_sem=ps_sem, recv_sem=pr_sem,
        device_id=(2 * z + 1 - core, e), device_id_type=MESH)
    to_core.start()
    legendre(core, put_b)
    to_core.wait_recv()
    z_copies = []
    for i in (2, 1, 3):
        kk = lax.rem(z + i, 4)
        zsend[i - 1] = (alm_b[kk] + pair[kk].astype(F32)).astype(BF16)
        copy = pltpu.make_async_remote_copy(
            src_ref=zsend.at[i - 1], dst_ref=zrecv.at[i - 1],
            send_sem=zs_sem.at[i - 1], recv_sem=zr_sem.at[i - 1],
            device_id=(2 * kk + core, e), device_id_type=MESH)
        copy.start()
        z_copies.append(copy)
    total[...] = alm_b[z] + pair[z].astype(F32)
    for copy in z_copies:
        copy.wait_recv()
    summed = total[...] + zrecv[0].astype(F32) + zrecv[1].astype(F32) + zrecv[2].astype(F32)

    for d in range(NM):
        asend[d, 0:24, :] = summed[24 * d : 24 * d + 24, :].astype(BF16)
        asend[d, 24:32, :] = jnp.zeros((8, 128), BF16)
    a_copies = []
    for i in range(1, NM):
        to = lax.rem(e + i, NM)
        copy = pltpu.make_async_remote_copy(
            src_ref=asend.at[to], dst_ref=arecv.at[e], send_sem=as_sem.at[i], recv_sem=ar_sem.at[e],
            device_id=(p, to), device_id_type=MESH)
        copy.start()
        a_copies.append(copy)
    arecv[e] = asend[e]
    for i in range(1, NM):
        src = lax.rem(e + NM - i, NM)
        pltpu.make_async_remote_copy(
            src_ref=arecv.at[src], dst_ref=arecv.at[src], send_sem=as_sem.at[0], recv_sem=ar_sem.at[src],
            device_id=(p, e), device_id_type=MESH).wait_recv()
    loads[9].wait()
    parts = arecv[...].astype(F32)
    alm = jnp.concatenate(
        [parts[:, 8 * gl : 8 * gl + 8, :].reshape(128, 128) for gl in range(3)], axis=1).astype(BF16)
    mixed = dot(ce[0], alm) + dot(ce[1], alm)
    scaled = (mixed * band[...]).astype(BF16)
    sketch = dot(scaled[:64], tt[:384, :]) + dot(scaled[64:], tt[384:, :])

    chunk = iota2((16, 128), 1) >> 5
    for tile in range(4):
        piece = [sketch[16 * q : 16 * q + 16, 128 * tile : 128 * tile + 128] for q in range(4)]
        for s in range(4):
            message = jnp.zeros((16, 128), F32)
            for q in range(4):
                shift = (32 * (q - s)) % 128
                moved_piece = piece[q] if shift == 0 else pltpu.roll(piece[q], shift, 1)
                message = jnp.where(chunk == q, moved_piece, message)
            fsend[4 * tile + s] = message
    f_copies = []
    for i in range(1, NM):
        to = lax.rem(e + i, NM)
        copy = pltpu.make_async_remote_copy(
            src_ref=fsend.at[to], dst_ref=frecv.at[e], send_sem=fs_sem.at[i], recv_sem=fr_sem.at[e],
            device_id=(p, to), device_id_type=MESH)
        copy.start()
        f_copies.append(copy)
    frecv[e] = fsend[e]
    for i in range(1, NM):
        src = lax.rem(e + NM - i, NM)
        pltpu.make_async_remote_copy(
            src_ref=frecv.at[src], dst_ref=frecv.at[src], send_sem=fs_sem.at[0], recv_sem=fr_sem.at[src],
            device_id=(p, e), device_id_type=MESH).wait_recv()
    gsend[...] = jnp.sum(frecv[...], axis=0)
    g_copies = []
    for i in range(1, NP):
        to = lax.rem(p + i, NP)
        copy = pltpu.make_async_remote_copy(
            src_ref=gsend, dst_ref=grecv.at[p], send_sem=gs_sem.at[i], recv_sem=gr_sem.at[p],
            device_id=(to, e), device_id_type=MESH)
        copy.start()
        g_copies.append(copy)
    grecv[p] = gsend[...]
    for i in range(1, NP):
        src = lax.rem(p + NP - i, NP)
        pltpu.make_async_remote_copy(
            src_ref=grecv.at[src], dst_ref=grecv.at[src], send_sem=gs_sem.at[0], recv_sem=gr_sem.at[src],
            device_id=(p, e), device_id_type=MESH).wait_recv()
    whole = jnp.sum(grecv[...], axis=0)
    for q in range(4):
        turned = pltpu.roll(whole, lax.rem(256 - 32 * q - 4 * p, 128), 1)
        out[16 * q : 16 * q + 16, :] = turned[:, :4]

    for i in range(1, NM):
        send_x(i).wait_send()
        send_l(i).wait_send()
    to_core.wait_send()
    for copy in z_copies + a_copies + f_copies + g_copies:
        copy.wait_send()


def local(sky_map, pixel_mask, noise_factor, cycle_legendre, band_power, channel_cov, test_matrix):
    wa, wb, twc, tws = fourier_tables()
    args = (
        jnp.transpose(sky_map, (0, 2, 1)).reshape(512, 512),
        pixel_mask,
        noise_factor.reshape(512, 64),
        jnp.transpose(cycle_legendre, (0, 2, 1)).reshape(64, 384),
        jnp.transpose(band_power),
        channel_cov,
        test_matrix.reshape(384, 2, 512),
        wa, wb, twc, tws,
    )
    dma = pltpu.SemaphoreType.DMA
    return pl.pallas_call(
        kernel,
        out_shape=jax.ShapeDtypeStruct((64, 4), F32),
        in_specs=[pl.BlockSpec(memory_space=pl.ANY)] * len(args),
        out_specs=pl.BlockSpec(memory_space=pltpu.VMEM),
        scratch_shapes=[
            pltpu.VMEM((512, 512), BF16),
            pltpu.VMEM((8, 512), jnp.int32),
            pltpu.VMEM((512, 64), F32),
            pltpu.VMEM((64, 384), F32),
            pltpu.VMEM((1, 384), F32),
            pltpu.VMEM((64, 64), F32),
            pltpu.VMEM((384, 2, 512), BF16),
            pltpu.VMEM((128, 64), BF16),
            pltpu.VMEM((384, 512), BF16),
            pltpu.VMEM((128, 128), F32),
            pltpu.VMEM((128, 128), F32),
            pltpu.VMEM((512, 512), BF16),
            pltpu.VMEM((16, 32, 512), BF16),
            pltpu.VMEM((16, 32, 512), BF16),
            pltpu.VMEM((2048, 128), F32),
            pltpu.VMEM((3, 64, 128), BF16),
            pltpu.VMEM((16, 3, 64, 128), BF16),
            pltpu.VMEM((3072, 128), F32),
            pltpu.VMEM((8, 384, 128), F32),
            pltpu.VMEM((4, 384, 128), BF16),
            pltpu.VMEM((4, 384, 128), F32),
            pltpu.VMEM((4, 384, 128), BF16),
            pltpu.VMEM((3, 384, 128), BF16),
            pltpu.VMEM((3, 384, 128), BF16),
            pltpu.VMEM((384, 128), F32),
            pltpu.VMEM((16, 32, 128), BF16),
            pltpu.VMEM((16, 32, 128), BF16),
            pltpu.VMEM((768, 512), BF16),
            pltpu.VMEM((2, 128, 128), BF16),
            pltpu.VMEM((16, 16, 128), F32),
            pltpu.VMEM((16, 16, 128), F32),
            pltpu.VMEM((16, 128), F32),
            pltpu.VMEM((8, 16, 128), F32),
            dma((11,)),
            dma((16,)), dma((16,)), dma((16,)), dma((16,)),
            dma, dma, dma((3,)), dma((3,)),
            dma((16,)), dma((16,)), dma((16,)), dma((16,)), dma((8,)), dma((8,)),
        ],
        compiler_params=pltpu.CompilerParams(collective_id=0, has_side_effects=True),
        name="harmonic_sketch",
    )(*args)


def solution(mesh):
    return jax.shard_map(
        local,
        mesh=mesh,
        in_specs=(
            P("patch", "mode", None),
            P("patch", "mode"),
            P("patch", "mode", None, None),
            P("patch", "mode", None),
            P("mode", "patch"),
            P(),
            P("patch", "mode", None, None),
        ),
        out_specs=P(None, ("patch", "mode")),
        check_vma=False,
    )
```

```python
import functools
import math

import jax
import jax.numpy as jnp
import numpy as np
from jax import lax
from jax.experimental import pallas as pl
from jax.experimental.pallas import tpu as pltpu
from jax.sharding import PartitionSpec as P

F32 = jnp.float32
BF16 = jnp.bfloat16
MESH = pl.DeviceIdType.MESH
NM = 16
NP = 8


def fourier_tables():
    m1 = np.arange(64)[:, None]
    j1 = np.arange(64)[None, :]
    angle = 2.0 * math.pi * ((m1 * j1) % 64) / 64.0
    wa = np.concatenate([np.cos(angle), -np.sin(angle)], axis=0)
    low = np.arange(128)[:, None]
    j2 = np.arange(128)[None, :]
    turn = 2.0 * math.pi * (low * j2) / 8192.0
    wb = np.zeros((48, 2, 4, 4, 2, 64))
    g = np.arange(48)[:, None]
    fold = np.arange(64)[None, :]
    phi = 2.0 * math.pi * ((g * fold) % 64) / 64.0
    for dd in range(4):
        wb[:, 0, dd, dd, 0, :] = np.cos(phi)
        wb[:, 0, dd, dd, 1, :] = np.sin(phi)
        wb[:, 1, dd, dd, 0, :] = -np.sin(phi)
        wb[:, 1, dd, dd, 1, :] = np.cos(phi)
    return (
        jnp.asarray(wa.astype(np.float32), BF16),
        jnp.asarray(wb.reshape(384, 512).astype(np.float32), BF16),
        jnp.asarray(np.cos(turn), F32),
        jnp.asarray(np.sin(turn), F32),
    )


def iota2(shape, axis):
    return lax.broadcasted_iota(jnp.int32, shape, axis)


def onehot(test):
    return jnp.where(test, 1.0, 0.0).astype(BF16)


def dot(a, b):
    return jnp.dot(a, b, preferred_element_type=F32)


def dot_nt(a, b):
    return lax.dot_general(a, b, (((1,), (1,)), ((), ())), preferred_element_type=F32)


def kernel(
    sky_h, mask_h, noise_h, leg_h, band_h, cov_h, test_h, wa_h, wb_h, twc_h, tws_h,
    out,
    sky, mask, noise, leg, band, cov, test, wa, wb, twc, tws,
    bd, xsend, xrecv, xs, lown, lall, lf, four, alm_a, alm_b, pair, zsend, zrecv,
    total, asend, arecv, tt, ce, fsend, frecv, gsend, grecv, turned,
    in_sem, xs_sem, xr_sem, ls_sem, lf_sem, lr_sem, ps_sem, pr_sem, zs_sem, zr_sem,
    as_sem, ar_sem, fs_sem, fr_sem, gs_sem, gr_sem,
):
    p = lax.axis_index("patch")
    e = lax.axis_index("mode")
    core = lax.rem(p, 2)
    z = p // 2
    ex = e // 4
    ey = lax.rem(e, 4)

    def ahead(a, b):
        return lax.rem(ex + a, 4) * 4 + lax.rem(ey + b, 4)

    def behind(a, b):
        return lax.rem(ex + 4 - a, 4) * 4 + lax.rem(ey + 4 - b, 4)

    barrier = pltpu.get_barrier_semaphore()
    for i in range(1, NM):
        pl.semaphore_signal(barrier, inc=1, device_id=(p, lax.rem(e + i, NM)), device_id_type=MESH)
    for i in range(1, NP):
        pl.semaphore_signal(barrier, inc=1, device_id=(lax.rem(p + i, NP), e), device_id_type=MESH)

    hbm = (noise_h, sky_h, mask_h, leg_h, wa_h, twc_h, tws_h, wb_h, cov_h, band_h, test_h)
    vmem = (noise, sky, mask, leg, wa, twc, tws, wb, cov, band, test)
    loads = [pltpu.make_async_copy(a, b, in_sem.at[i]) for i, (a, b) in enumerate(zip(hbm, vmem))]
    for load in loads:
        load.start()

    row = iota2((512, 512), 0)
    lane = iota2((512, 512), 1)
    source = ((row >> 2) & 7) * 64 + (row >> 5) * 4 + (row & 3)
    order = onehot(lane == source)
    repeat = onehot((iota2((64, 512), 1) & 63) == iota2((64, 512), 0))
    loads[0].wait()
    moved = dot(order, noise[...].astype(BF16)).astype(BF16)
    wide = dot(moved, repeat)
    bd[...] = jnp.where((lane >> 6) == ((row >> 2) & 7), wide, 0.0).astype(BF16)
    loads[1].wait()
    loads[2].wait()
    for r in range(8):
        seen = jnp.broadcast_to(mask[r : r + 1, :].astype(F32), (64, 512)).astype(BF16)
        sky[64 * r : 64 * r + 64, :] = sky[64 * r : 64 * r + 64, :] * seen

    loads[3].wait()
    for h in range(2):
        for t in range(3):
            lown[h, t] = leg[32 * h : 32 * h + 32, 128 * t : 128 * t + 128].astype(BF16)

    def send_x(a, b):
        to = ahead(a, b)
        return pltpu.make_async_remote_copy(
            src_ref=xsend.at[to], dst_ref=xrecv.at[e], send_sem=xs_sem.at[4 * a + b], recv_sem=xr_sem.at[e],
            device_id=(p, to), device_id_type=MESH)

    def send_l(a, b):
        return pltpu.make_async_remote_copy(
            src_ref=lown, dst_ref=lall.at[4 * a + b], send_sem=ls_sem.at[a, b], recv_sem=lr_sem.at[4 * a + b, 0],
            device_id=(p, ahead(a, b)), device_id_type=MESH)

    def relay_l(a, b, h):
        source, to = ((4 * a, ahead(0, b)), (b, ahead(a, 0)))[h]
        return pltpu.make_async_remote_copy(
            src_ref=lall.at[source, h], dst_ref=lall.at[4 * a + b, h],
            send_sem=lf_sem.at[4 * a + b, h], recv_sem=lr_sem.at[4 * a + b, h],
            device_id=(p, to), device_id_type=MESH)

    straight = [(0, 2), (2, 0), (0, 1), (0, 3), (1, 0), (3, 0)]
    relayed = [(a, b) for a in range(1, 4) for b in range(1, 4)]

    pl.semaphore_wait(barrier, NM - 1 + NP - 1)
    for a, b in straight:
        send_l(a, b).start()
    for n in range(4):
        q = lax.rem(ex + n, 4)
        white = dot(bd[pl.ds(pl.multiple_of(128 * q, 128), 128), :], sky[...]).astype(BF16)
        xsend[pl.ds(4 * q, 4)] = white.reshape(4, 32, 512)
        for b in range(4):
            if n + b > 0:
                send_x(n, b).start()

    loads[10].wait()
    loads[8].wait()
    split = onehot(iota2((256, 256), 1) == 2 * (iota2((256, 256), 0) & 127) + (iota2((256, 256), 0) >> 7))
    s_to = iota2((512, 512), 1)
    s_from = ((s_to >> 2) & 7) * 64 + (s_to >> 5) * 4 + (s_to & 3)
    columns = onehot(iota2((512, 512), 0) == s_from)
    for b in range(3):
        block = test[128 * b : 128 * b + 128].reshape(256, 512)
        parts = dot(dot(split, block).astype(BF16), columns).astype(BF16)
        tt[128 * b : 128 * b + 128, :] = parts[:128]
        tt[384 + 128 * b : 384 + 128 * b + 128, :] = parts[128:]
    l128 = iota2((64, 128), 1)
    spread = onehot(iota2((64, 128), 0) == 4 * (l128 >> 3) + (l128 & 3))
    high = cov[...].astype(BF16)
    rest = (cov[...] - high.astype(F32)).astype(BF16)
    for n, piece in enumerate((high, rest)):
        wide_cov = dot(piece, spread)
        for t in range(2):
            ce[n, 64 * t : 64 * t + 64, :] = jnp.where(((l128 >> 2) & 1) == t, wide_cov, 0.0).astype(BF16)

    def wait_x(src):
        pltpu.make_async_remote_copy(
            src_ref=xrecv.at[src], dst_ref=xrecv.at[src], send_sem=xs_sem.at[0], recv_sem=xr_sem.at[src],
            device_id=(p, e), device_id_type=MESH).wait_recv()

    def wait_l(slot, h=None):
        ref = lall.at[slot] if h is None else lall.at[slot, h]
        pltpu.make_async_remote_copy(
            src_ref=ref, dst_ref=ref, send_sem=lf_sem.at[0, 0], recv_sem=lr_sem.at[slot, 0 if h is None else h],
            device_id=(p, e), device_id_type=MESH).wait_recv()

    def spread_x(ref, src):
        for h in range(4):
            xs[pl.ds(src * 4 + h, 32, stride=64), :] = ref[src, :, 128 * h : 128 * h + 128].astype(F32)

    def spread_l(ref, slot):
        for h in range(2):
            for t in range(3):
                lf[192 * slot + 64 * t + 32 * h : 192 * slot + 64 * t + 32 * h + 32, :] = ref[h, t].astype(F32)

    for n in (1, 3, 2):
        wait_l(4 * n)
        for b in (2, 1, 3):
            relay_l(n, b, 0).start()
        wait_l(n)
        for a in (2, 1, 3):
            relay_l(a, n, 1).start()

    spread_x(xsend, e)
    spread_l(lown, 0)
    for a, b in straight:
        spread_l(lall.at[4 * a + b], 4 * a + b)

    def take_x(i, carry):
        src = lax.rem(e + NM - i, NM)
        wait_x(src)
        spread_x(xrecv, src)
        return carry

    lax.fori_loop(1, NM, take_x, 0)

    loads[4].wait()
    loads[5].wait()
    loads[6].wait()
    loads[7].wait()
    left_half = iota2((64, 128), 1) < 64

    def transform(pair_index, carry):
        rows = []
        for s in range(2):
            base = pair_index * 512 + s * 256
            pix = [xs[pl.ds(pl.multiple_of(base + 64 * dd, 64), 64), :] for dd in range(4)]
            first = dot(wa[...], jnp.concatenate(pix, axis=1).astype(BF16))
            lanes = []
            for dd in range(4):
                re = first[:64, 128 * dd : 128 * dd + 128]
                im = first[64:, 128 * dd : 128 * dd + 128]
                halves = []
                for h in range(2):
                    c = twc[64 * h : 64 * h + 64, :]
                    sn = tws[64 * h : 64 * h + 64, :]
                    tr = re * c + im * sn
                    ti = im * c - re * sn
                    halves.append(
                        jnp.where(left_half, tr, ti) + pltpu.roll(jnp.where(left_half, ti, tr), 64, 1))
                lanes.append(jnp.concatenate(halves, axis=0).astype(BF16))
            rows.append(jnp.concatenate(lanes, axis=1))
        second = dot_nt(wb[...], jnp.concatenate(rows, axis=0))
        four[2 * pair_index] = second[:, :128]
        four[2 * pair_index + 1] = second[:, 128:]
        return carry

    lax.fori_loop(0, 4, transform, 0)

    def legendre(a, parity, put):
        def body(j, carry):
            acc = [[None, None] for _ in range(4)]
            for gi in range(2):
                q = 2 * j + gi
                b = q // 3
                g = 3 * (lax.rem(ex + 4 - a, 4) * 4 + lax.rem(ey + 4 - b, 4)) + q - 3 * b
                for r in range(8):
                    f = four[r, pl.ds(pl.multiple_of(g * 8, 8), 8), :]
                    for kk in range(4):
                        lrow = lf[pl.ds((12 * a + q) * 64 + r * 8 + 2 * kk + parity, 8, stride=0), :]
                        term = lrow * f
                        acc[kk][gi] = term if r == 0 else acc[kk][gi] + term
            for kk in range(4):
                put(kk, pl.ds(pl.multiple_of(j * 16, 16), 16), jnp.concatenate(acc[kk], axis=0))
            return carry

        lax.fori_loop(0, 6, body, 0)

    def to_core(n):
        return pltpu.make_async_remote_copy(
            src_ref=alm_a.at[n], dst_ref=pair.at[n], send_sem=ps_sem.at[n], recv_sem=pr_sem.at[n],
            device_id=(2 * z + 1 - core, e), device_id_type=MESH)

    def to_chip(n, i):
        return pltpu.make_async_remote_copy(
            src_ref=zsend.at[n, i - 1], dst_ref=zrecv.at[n, i - 1],
            send_sem=zs_sem.at[n, i - 1], recv_sem=zr_sem.at[n, i - 1],
            device_id=(2 * lax.rem(z + i, 4) + core, e), device_id_type=MESH)

    def to_owner(n, b):
        return pltpu.make_async_remote_copy(
            src_ref=asend.at[n, b], dst_ref=arecv.at[e], send_sem=as_sem.at[n, b], recv_sem=ar_sem.at[e],
            device_id=(p, behind(n, b)), device_id_type=MESH)

    def group_terms(n):
        for b in range(4):
            if n > 0 and b > 0:
                for h in range(2):
                    wait_l(4 * n + b, h)
                spread_l(lall.at[4 * n + b], 4 * n + b)

        def put_a(kk, rows, value):
            alm_a[n, kk, rows, :] = value.astype(BF16)

        def put_b(kk, rows, value):
            alm_b[n, kk, rows, :] = value

        legendre(n, 1 - core, put_a)
        to_core(n).start()
        legendre(n, core, put_b)

    def group_pair(n):
        to_core(n).wait_recv()
        for i in (2, 1, 3):
            kk = lax.rem(z + i, 4)
            zsend[n, i - 1] = (alm_b[n, kk] + pair[n, kk].astype(F32)).astype(BF16)
            to_chip(n, i).start()
        total[n] = alm_b[n, z] + pair[n, z].astype(F32)

    def group_return(n):
        for i in (1, 3, 2):
            to_chip(n, i).wait_recv()
        summed = total[n] + zrecv[n, 0].astype(F32) + zrecv[n, 1].astype(F32) + zrecv[n, 2].astype(F32)
        for b in range(4):
            asend[n, b, 0:24, :] = summed[24 * b : 24 * b + 24, :].astype(BF16)
            asend[n, b, 24:32, :] = jnp.zeros((8, 128), BF16)
            if n + b > 0:
                to_owner(n, b).start()
        if n == 0:
            arecv[e] = asend[0, 0]

    for n in range(6):
        if n < 4:
            group_terms(n)
        if 1 <= n <= 4:
            group_pair(n - 1)
        if n >= 2:
            group_return(n - 2)

    for i in range(1, NM):
        src = lax.rem(e + NM - i, NM)
        pltpu.make_async_remote_copy(
            src_ref=arecv.at[src], dst_ref=arecv.at[src], send_sem=as_sem.at[0, 0], recv_sem=ar_sem.at[src],
            device_id=(p, e), device_id_type=MESH).wait_recv()
    loads[9].wait()
    parts = arecv[...].astype(F32)
    alm = jnp.concatenate(
        [parts[:, 8 * gl : 8 * gl + 8, :].reshape(128, 128) for gl in range(3)], axis=1).astype(BF16)
    mixed = dot(ce[0], alm) + dot(ce[1], alm)
    scaled = (mixed * band[...]).astype(BF16)
    sketch = dot(scaled[:64], tt[:384, :]) + dot(scaled[64:], tt[384:, :])

    chunk = iota2((16, 128), 1) >> 5
    for tile in range(4):
        piece = [sketch[16 * q : 16 * q + 16, 128 * tile : 128 * tile + 128] for q in range(4)]
        for s in range(4):
            message = jnp.zeros((16, 128), F32)
            for q in range(4):
                shift = (32 * (q - s)) % 128
                moved_piece = piece[q] if shift == 0 else pltpu.roll(piece[q], shift, 1)
                message = jnp.where(chunk == q, moved_piece, message)
            fsend[4 * tile + s] = message
    f_copies = []
    for i in range(1, NM):
        to = lax.rem(e + i, NM)
        copy = pltpu.make_async_remote_copy(
            src_ref=fsend.at[to], dst_ref=frecv.at[e], send_sem=fs_sem.at[i], recv_sem=fr_sem.at[e],
            device_id=(p, to), device_id_type=MESH)
        copy.start()
        f_copies.append(copy)
    frecv[e] = fsend[e]
    for i in range(1, NM):
        src = lax.rem(e + NM - i, NM)
        pltpu.make_async_remote_copy(
            src_ref=frecv.at[src], dst_ref=frecv.at[src], send_sem=fs_sem.at[0], recv_sem=fr_sem.at[src],
            device_id=(p, e), device_id_type=MESH).wait_recv()
    gsend[...] = jnp.sum(frecv[...], axis=0)
    g_copies = []
    for i in range(1, NP):
        to = lax.rem(p + i, NP)
        copy = pltpu.make_async_remote_copy(
            src_ref=gsend, dst_ref=grecv.at[p], send_sem=gs_sem.at[i], recv_sem=gr_sem.at[p],
            device_id=(to, e), device_id_type=MESH)
        copy.start()
        g_copies.append(copy)
    grecv[p] = gsend[...]
    for i in range(1, NP):
        src = lax.rem(p + NP - i, NP)
        pltpu.make_async_remote_copy(
            src_ref=grecv.at[src], dst_ref=grecv.at[src], send_sem=gs_sem.at[0], recv_sem=gr_sem.at[src],
            device_id=(p, e), device_id_type=MESH).wait_recv()
    whole = jnp.sum(grecv[...], axis=0)
    turned[...] = jnp.transpose(whole)
    out[...] = jnp.concatenate([turned[pl.ds(32 * q + 4 * p, 4), :] for q in range(4)], axis=1)

    for a in range(4):
        for b in range(4):
            if a + b > 0:
                send_x(a, b).wait_send()
                to_owner(a, b).wait_send()
    for a, b in straight:
        send_l(a, b).wait_send()
    for a, b in relayed:
        for h in range(2):
            relay_l(a, b, h).wait_send()
    for n in range(4):
        to_core(n).wait_send()
        for i in range(1, 4):
            to_chip(n, i).wait_send()
    for copy in f_copies + g_copies:
        copy.wait_send()


def local(sky_map, pixel_mask, noise_factor, cycle_legendre, band_power, channel_cov, test_matrix):
    wa, wb, twc, tws = fourier_tables()
    args = (
        jnp.transpose(sky_map, (0, 2, 1)).reshape(512, 512),
        pixel_mask,
        noise_factor.reshape(512, 64),
        jnp.transpose(cycle_legendre, (0, 2, 1)).reshape(64, 384),
        jnp.transpose(band_power),
        channel_cov,
        test_matrix.reshape(384, 2, 512),
        wa, wb, twc, tws,
    )
    dma = pltpu.SemaphoreType.DMA
    result = pl.pallas_call(
        kernel,
        out_shape=jax.ShapeDtypeStruct((4, 64), F32),
        in_specs=[pl.BlockSpec(memory_space=pl.ANY)] * len(args),
        out_specs=pl.BlockSpec(memory_space=pltpu.VMEM),
        scratch_shapes=[
            pltpu.VMEM((512, 512), BF16),
            pltpu.VMEM((8, 512), jnp.int32),
            pltpu.VMEM((512, 64), F32),
            pltpu.VMEM((64, 384), F32),
            pltpu.VMEM((1, 384), F32),
            pltpu.VMEM((64, 64), F32),
            pltpu.VMEM((384, 2, 512), BF16),
            pltpu.VMEM((128, 64), BF16),
            pltpu.VMEM((384, 512), BF16),
            pltpu.VMEM((128, 128), F32),
            pltpu.VMEM((128, 128), F32),
            pltpu.VMEM((512, 512), BF16),
            pltpu.VMEM((16, 32, 512), BF16),
            pltpu.VMEM((16, 32, 512), BF16),
            pltpu.VMEM((2048, 128), F32),
            pltpu.VMEM((2, 3, 32, 128), BF16),
            pltpu.VMEM((16, 2, 3, 32, 128), BF16),
            pltpu.VMEM((3072, 128), F32),
            pltpu.VMEM((8, 384, 128), F32),
            pltpu.VMEM((4, 4, 96, 128), BF16),
            pltpu.VMEM((4, 4, 96, 128), F32),
            pltpu.VMEM((4, 4, 96, 128), BF16),
            pltpu.VMEM((4, 3, 96, 128), BF16),
            pltpu.VMEM((4, 3, 96, 128), BF16),
            pltpu.VMEM((4, 96, 128), F32),
            pltpu.VMEM((4, 4, 32, 128), BF16),
            pltpu.VMEM((16, 32, 128), BF16),
            pltpu.VMEM((768, 512), BF16),
            pltpu.VMEM((2, 128, 128), BF16),
            pltpu.VMEM((16, 16, 128), F32),
            pltpu.VMEM((16, 16, 128), F32),
            pltpu.VMEM((16, 128), F32),
            pltpu.VMEM((8, 16, 128), F32),
            pltpu.VMEM((128, 16), F32),
            dma((11,)),
            dma((16,)), dma((16,)), dma((4, 4)), dma((16, 2)), dma((16, 2)),
            dma((4,)), dma((4,)), dma((4, 3)), dma((4, 3)),
            dma((4, 4)), dma((16,)), dma((16,)), dma((16,)), dma((8,)), dma((8,)),
        ],
        compiler_params=pltpu.CompilerParams(collective_id=0, has_side_effects=True),
        name="harmonic_sketch",
    )(*args)
    return jnp.transpose(result)


def solution(mesh):
    return jax.shard_map(
        local,
        mesh=mesh,
        in_specs=(
            P("patch", "mode", None),
            P("patch", "mode"),
            P("patch", "mode", None, None),
            P("patch", "mode", None),
            P("mode", "patch"),
            P(),
            P("patch", "mode", None, None),
        ),
        out_specs=P(None, ("patch", "mode")),
        check_vma=False,
    )
```

```python
import functools
import math

import jax
import jax.numpy as jnp
import numpy as np
from jax import lax
from jax.experimental import pallas as pl
from jax.experimental.pallas import tpu as pltpu
from jax.sharding import PartitionSpec as P

F32 = jnp.float32
BF16 = jnp.bfloat16
MESH = pl.DeviceIdType.MESH
NM = 16
RELAY_AT = 6


def fourier_tables():
    m1 = np.arange(64)[:, None]
    j1 = np.arange(64)[None, :]
    angle = 2.0 * math.pi * ((m1 * j1) % 64) / 64.0
    wa = np.concatenate([np.cos(angle), -np.sin(angle)], axis=0)
    low = np.arange(128)[:, None]
    j2 = np.arange(128)[None, :]
    turn = 2.0 * math.pi * (low * j2) / 8192.0
    wb = np.zeros((48, 2, 4, 4, 2, 64))
    g = np.arange(48)[:, None]
    fold = np.arange(64)[None, :]
    phi = 2.0 * math.pi * ((g * fold) % 64) / 64.0
    for dd in range(4):
        wb[:, 0, dd, dd, 0, :] = np.cos(phi)
        wb[:, 0, dd, dd, 1, :] = np.sin(phi)
        wb[:, 1, dd, dd, 0, :] = -np.sin(phi)
        wb[:, 1, dd, dd, 1, :] = np.cos(phi)
    return (
        jnp.asarray(wa.astype(np.float32), BF16),
        jnp.asarray(wb.reshape(384, 512).astype(np.float32), BF16),
        jnp.asarray(np.cos(turn), F32),
        jnp.asarray(np.sin(turn), F32),
    )


def iota2(shape, axis):
    return lax.broadcasted_iota(jnp.int32, shape, axis)


def onehot(test):
    return jnp.where(test, 1.0, 0.0).astype(BF16)


def dot(a, b):
    return jnp.dot(a, b, preferred_element_type=F32)


def dot_nt(a, b):
    return lax.dot_general(a, b, (((1,), (1,)), ((), ())), preferred_element_type=F32)


def kernel(
    sky_h, mask_h, noise_h, leg_h, band_h, cov_h, test_h, wa_h, wb_h, twc_h, tws_h,
    out,
    sky, mask, noise, leg, band, cov, test, wa, wb, twc, tws,
    bd, xsend, xrecv, xs, lown, lall, lf, four, alm_a, alm_b, pair, asend, arecv, tt, ce,
    ssend, srecv, fsend, frecv,
    in_sem, xs_sem, xr_sem, ls_sem, lf_sem, lr_sem, ps_sem, pr_sem,
    as_sem, ar_sem, ss_sem, sr_sem, fs_sem, fr_sem,
):
    p = lax.axis_index("patch")
    e = lax.axis_index("mode")
    core = lax.rem(p, 2)
    z = p // 2
    ex = e // 4
    ey = lax.rem(e, 4)

    def ahead(a, b):
        return lax.rem(ex + a, 4) * 4 + lax.rem(ey + b, 4)

    def behind(a, b):
        return lax.rem(ex + 4 - a, 4) * 4 + lax.rem(ey + 4 - b, 4)

    def plane(dz):
        return 2 * lax.rem(z + dz, 4) + core

    peers = [(dz, a, b) for dz in range(4) for a in range(4) for b in range(4) if dz + a + b > 0]
    peers.sort(key=lambda t: -sum(min(v, 4 - v) for v in t))

    barrier = pltpu.get_barrier_semaphore()
    pl.semaphore_signal(barrier, inc=1, device_id=(2 * z + 1 - core, e), device_id_type=MESH)
    for dz, a, b in peers:
        pl.semaphore_signal(barrier, inc=1, device_id=(plane(dz), ahead(a, b)), device_id_type=MESH)

    hbm = (noise_h, sky_h, mask_h, leg_h, wa_h, twc_h, tws_h, wb_h, cov_h, band_h, test_h)
    vmem = (noise, sky, mask, leg, wa, twc, tws, wb, cov, band, test)
    loads = [pltpu.make_async_copy(a, b, in_sem.at[i]) for i, (a, b) in enumerate(zip(hbm, vmem))]
    for load in loads:
        load.start()

    row = iota2((512, 512), 0)
    lane = iota2((512, 512), 1)
    source = ((row >> 2) & 7) * 64 + (row >> 5) * 4 + (row & 3)
    order = onehot(lane == source)
    repeat = onehot((iota2((64, 512), 1) & 63) == iota2((64, 512), 0))
    loads[0].wait()
    moved = dot(order, noise[...].astype(BF16)).astype(BF16)
    wide = dot(moved, repeat)
    bd[...] = jnp.where((lane >> 6) == ((row >> 2) & 7), wide, 0.0).astype(BF16)
    loads[1].wait()
    loads[2].wait()
    for r in range(8):
        seen = jnp.broadcast_to(mask[r : r + 1, :].astype(F32), (64, 512)).astype(BF16)
        sky[64 * r : 64 * r + 64, :] = sky[64 * r : 64 * r + 64, :] * seen

    loads[3].wait()
    for h in range(2):
        for t in range(3):
            lown[h, t] = leg[32 * h : 32 * h + 32, 128 * t : 128 * t + 128].astype(BF16)

    def send_x(a, b):
        to = ahead(a, b)
        return pltpu.make_async_remote_copy(
            src_ref=xsend.at[to], dst_ref=xrecv.at[e], send_sem=xs_sem.at[4 * a + b], recv_sem=xr_sem.at[e],
            device_id=(p, to), device_id_type=MESH)

    def send_l(a, b):
        return pltpu.make_async_remote_copy(
            src_ref=lown, dst_ref=lall.at[4 * a + b], send_sem=ls_sem.at[a, b], recv_sem=lr_sem.at[4 * a + b, 0],
            device_id=(p, ahead(a, b)), device_id_type=MESH)

    def relay_l(a, b, h):
        source, to = ((4 * a, ahead(0, b)), (b, ahead(a, 0)))[h]
        return pltpu.make_async_remote_copy(
            src_ref=lall.at[source, h], dst_ref=lall.at[4 * a + b, h],
            send_sem=lf_sem.at[4 * a + b, h], recv_sem=lr_sem.at[4 * a + b, h],
            device_id=(p, to), device_id_type=MESH)

    straight = [(0, 2), (2, 0), (0, 1), (0, 3), (1, 0), (3, 0)]
    relayed = [(a, b) for a in range(1, 4) for b in range(1, 4)]

    pl.semaphore_wait(barrier, len(peers) + 1)
    for a, b in straight:
        send_l(a, b).start()
    for n in range(4):
        q = lax.rem(ex + n, 4)
        white = dot(bd[pl.ds(pl.multiple_of(128 * q, 128), 128), :], sky[...]).astype(BF16)
        xsend[pl.ds(4 * q, 4)] = white.reshape(4, 32, 512)
        for b in range(4):
            if n + b > 0:
                send_x(n, b).start()

    loads[10].wait()
    loads[8].wait()
    split = onehot(iota2((256, 256), 1) == 2 * (iota2((256, 256), 0) & 127) + (iota2((256, 256), 0) >> 7))
    to = iota2((256, 512), 0)
    wanted = ((to >> 5) & 3) * 128 + (to >> 7) * 64 + ((to >> 1) & 15) * 4 + (to & 1) * 2
    columns = [onehot(iota2((256, 512), 1) == wanted + h) for h in range(2)]
    for b in range(3):
        block = dot(split, test[128 * b : 128 * b + 128].reshape(256, 512)).astype(BF16)
        for h in range(2):
            parts = dot_nt(columns[h], block).astype(BF16)
            tt[h, :, 128 * b : 128 * b + 128] = parts[:, :128]
            tt[h, :, 384 + 128 * b : 384 + 128 * b + 128] = parts[:, 128:]
    l128 = iota2((64, 128), 1)
    spread = onehot(iota2((64, 128), 0) == 4 * (l128 >> 3) + (l128 & 3))
    high = cov[...].astype(BF16)
    rest = (cov[...] - high.astype(F32)).astype(BF16)
    for n, piece in enumerate((high, rest)):
        wide_cov = dot(piece, spread)
        for t in range(2):
            ce[n, 64 * t : 64 * t + 64, :] = jnp.where(((l128 >> 2) & 1) == t, wide_cov, 0.0).astype(BF16)

    def wait_x(src):
        pltpu.make_async_remote_copy(
            src_ref=xrecv.at[src], dst_ref=xrecv.at[src], send_sem=xs_sem.at[0], recv_sem=xr_sem.at[src],
            device_id=(p, e), device_id_type=MESH).wait_recv()

    def wait_l(slot, h=None):
        ref = lall.at[slot] if h is None else lall.at[slot, h]
        pltpu.make_async_remote_copy(
            src_ref=ref, dst_ref=ref, send_sem=lf_sem.at[0, 0], recv_sem=lr_sem.at[slot, 0 if h is None else h],
            device_id=(p, e), device_id_type=MESH).wait_recv()

    def spread_x(ref, src):
        for h in range(4):
            xs[pl.ds(src * 4 + h, 32, stride=64), :] = ref[src, :, 128 * h : 128 * h + 128].astype(F32)

    def spread_l(ref, slot):
        for h in range(2):
            for t in range(3):
                lf[192 * slot + 64 * t + 32 * h : 192 * slot + 64 * t + 32 * h + 32, :] = ref[h, t].astype(F32)

    def take_x(i, carry):
        src = lax.rem(e + NM - i, NM)
        wait_x(src)
        spread_x(xrecv, src)
        return carry

    spread_x(xsend, e)
    spread_l(lown, 0)
    lax.fori_loop(1, RELAY_AT, take_x, 0)
    for n in (1, 3, 2):
        wait_l(4 * n)
        for b in (2, 1, 3):
            relay_l(n, b, 0).start()
        wait_l(n)
        for a in (2, 1, 3):
            relay_l(a, n, 1).start()
    lax.fori_loop(RELAY_AT, NM, take_x, 0)
    for a, b in straight:
        spread_l(lall.at[4 * a + b], 4 * a + b)

    loads[4].wait()
    loads[5].wait()
    loads[6].wait()
    loads[7].wait()
    left_half = iota2((64, 128), 1) < 64

    def transform(pair_index, carry):
        rows = []
        for s in range(2):
            base = pair_index * 512 + s * 256
            pix = [xs[pl.ds(pl.multiple_of(base + 64 * dd, 64), 64), :] for dd in range(4)]
            first = dot(wa[...], jnp.concatenate(pix, axis=1).astype(BF16))
            lanes = []
            for dd in range(4):
                re = first[:64, 128 * dd : 128 * dd + 128]
                im = first[64:, 128 * dd : 128 * dd + 128]
                halves = []
                for h in range(2):
                    c = twc[64 * h : 64 * h + 64, :]
                    sn = tws[64 * h : 64 * h + 64, :]
                    tr = re * c + im * sn
                    ti = im * c - re * sn
                    halves.append(
                        jnp.where(left_half, tr, ti) + pltpu.roll(jnp.where(left_half, ti, tr), 64, 1))
                lanes.append(jnp.concatenate(halves, axis=0).astype(BF16))
            rows.append(jnp.concatenate(lanes, axis=1))
        second = dot_nt(wb[...], jnp.concatenate(rows, axis=0))
        four[2 * pair_index] = second[:, :128]
        four[2 * pair_index + 1] = second[:, 128:]
        return carry

    lax.fori_loop(0, 4, transform, 0)

    def legendre(a, parity, put):
        def body(j, carry):
            acc = [[None, None] for _ in range(4)]
            for gi in range(2):
                q = 2 * j + gi
                b = q // 3
                g = 3 * (lax.rem(ex + 4 - a, 4) * 4 + lax.rem(ey + 4 - b, 4)) + q - 3 * b
                for r in range(8):
                    f = four[r, pl.ds(pl.multiple_of(g * 8, 8), 8), :]
                    for kk in range(4):
                        lrow = lf[pl.ds((12 * a + q) * 64 + r * 8 + 2 * kk + parity, 8, stride=0), :]
                        term = lrow * f
                        acc[kk][gi] = term if r == 0 else acc[kk][gi] + term
            for kk in range(4):
                put(kk, pl.ds(pl.multiple_of(j * 16, 16), 16), jnp.concatenate(acc[kk], axis=0))
            return carry

        lax.fori_loop(0, 6, body, 0)

    def to_core(n):
        return pltpu.make_async_remote_copy(
            src_ref=alm_a.at[n], dst_ref=pair.at[n], send_sem=ps_sem.at[n], recv_sem=pr_sem.at[n],
            device_id=(2 * z + 1 - core, e), device_id_type=MESH)

    def to_owner(dz, n, b):
        return pltpu.make_async_remote_copy(
            src_ref=asend.at[n, dz, b], dst_ref=arecv.at[dz, e],
            send_sem=as_sem.at[n, 4 * dz + b], recv_sem=ar_sem.at[dz, e],
            device_id=(plane(dz), behind(n, b)), device_id_type=MESH)

    def group_terms(n):
        for b in range(4):
            if n > 0 and b > 0:
                for h in range(2):
                    wait_l(4 * n + b, h)
                spread_l(lall.at[4 * n + b], 4 * n + b)

        def put_a(kk, rows, value):
            alm_a[n, kk, rows, :] = value.astype(BF16)

        def put_b(kk, rows, value):
            alm_b[n, kk, rows, :] = value

        legendre(n, 1 - core, put_a)
        to_core(n).start()
        legendre(n, core, put_b)

    def group_pair(n):
        to_core(n).wait_recv()
        for dz in (2, 1, 3, 0):
            kk = lax.rem(z + dz, 4)
            both = (alm_b[n, kk] + pair[n, kk].astype(F32)).astype(BF16)
            for b in (2, 1, 3, 0):
                asend[n, dz, b] = both[24 * b : 24 * b + 24, :]
                if dz + n + b > 0:
                    to_owner(dz, n, b).start()

    for n in range(5):
        if n < 4:
            group_terms(n)
        if n > 0:
            group_pair(n - 1)
    arecv[0, e] = asend[0, 0, 0]
    for dz, a, b in reversed(peers):
        ref = arecv.at[dz, behind(a, b)]
        pltpu.make_async_remote_copy(
            src_ref=ref, dst_ref=ref, send_sem=as_sem.at[0, 0], recv_sem=ar_sem.at[dz, behind(a, b)],
            device_id=(p, e), device_id_type=MESH).wait_recv()
    loads[9].wait()
    parts = arecv[0].astype(F32) + arecv[1].astype(F32) + arecv[2].astype(F32) + arecv[3].astype(F32)
    alm = jnp.concatenate(
        [parts[:, 8 * gl : 8 * gl + 8, :].reshape(128, 128) for gl in range(3)], axis=1).astype(BF16)
    mixed = dot(ce[0], alm) + dot(ce[1], alm)
    scaled = (mixed * band[...]).astype(BF16)
    scaled = jnp.concatenate([scaled[:64], scaled[64:]], axis=1)
    sketch = jnp.concatenate([dot_nt(tt[h], scaled) for h in range(2)], axis=1)
    ssend[...] = sketch.reshape(2, 64, 2, 128)

    to_sibling = pltpu.make_async_remote_copy(
        src_ref=ssend.at[1 - core], dst_ref=srecv, send_sem=ss_sem, recv_sem=sr_sem,
        device_id=(2 * z + 1 - core, e), device_id_type=MESH)
    to_sibling.start()
    to_sibling.wait_recv()
    fsend[...] = ssend[core] + srecv[...]

    def to_column(dz, a, b):
        column = lax.rem(z + dz, 4) * 16 + ahead(a, b)
        return pltpu.make_async_remote_copy(
            src_ref=fsend.at[column], dst_ref=frecv.at[16 * z + e],
            send_sem=fs_sem.at[16 * dz + 4 * a + b], recv_sem=fr_sem.at[16 * z + e],
            device_id=(plane(dz), ahead(a, b)), device_id_type=MESH)

    for dz, a, b in peers:
        to_column(dz, a, b).start()
    frecv[16 * z + e] = fsend[16 * z + e]
    for dz, a, b in reversed(peers):
        source = lax.rem(z + 4 - dz, 4) * 16 + behind(a, b)
        ref = frecv.at[source]
        pltpu.make_async_remote_copy(
            src_ref=ref, dst_ref=ref, send_sem=fs_sem.at[0], recv_sem=fr_sem.at[source],
            device_id=(p, e), device_id_type=MESH).wait_recv()
    out[...] = jnp.sum(frecv[...], axis=0)

    for a in range(4):
        for b in range(4):
            if a + b > 0:
                send_x(a, b).wait_send()
    for a, b in straight:
        send_l(a, b).wait_send()
    for a, b in relayed:
        for h in range(2):
            relay_l(a, b, h).wait_send()
    for n in range(4):
        to_core(n).wait_send()
    for dz, a, b in peers:
        to_owner(dz, a, b).wait_send()
        to_column(dz, a, b).wait_send()
    to_sibling.wait_send()


def local(sky_map, pixel_mask, noise_factor, cycle_legendre, band_power, channel_cov, test_matrix):
    wa, wb, twc, tws = fourier_tables()
    args = (
        jnp.transpose(sky_map, (0, 2, 1)).reshape(512, 512),
        pixel_mask,
        noise_factor.reshape(512, 64),
        jnp.transpose(cycle_legendre, (0, 2, 1)).reshape(64, 384),
        jnp.transpose(band_power),
        channel_cov,
        test_matrix.reshape(384, 2, 512),
        wa, wb, twc, tws,
    )
    dma = pltpu.SemaphoreType.DMA
    result = pl.pallas_call(
        kernel,
        out_shape=jax.ShapeDtypeStruct((2, 128), F32),
        in_specs=[pl.BlockSpec(memory_space=pl.ANY)] * len(args),
        out_specs=pl.BlockSpec(memory_space=pltpu.VMEM),
        scratch_shapes=[
            pltpu.VMEM((512, 512), BF16),
            pltpu.VMEM((8, 512), jnp.int32),
            pltpu.VMEM((512, 64), F32),
            pltpu.VMEM((64, 384), F32),
            pltpu.VMEM((1, 384), F32),
            pltpu.VMEM((64, 64), F32),
            pltpu.VMEM((384, 2, 512), BF16),
            pltpu.VMEM((128, 64), BF16),
            pltpu.VMEM((384, 512), BF16),
            pltpu.VMEM((128, 128), F32),
            pltpu.VMEM((128, 128), F32),
            pltpu.VMEM((512, 512), BF16),
            pltpu.VMEM((16, 32, 512), BF16),
            pltpu.VMEM((16, 32, 512), BF16),
            pltpu.VMEM((2048, 128), F32),
            pltpu.VMEM((2, 3, 32, 128), BF16),
            pltpu.VMEM((16, 2, 3, 32, 128), BF16),
            pltpu.VMEM((3072, 128), F32),
            pltpu.VMEM((8, 384, 128), F32),
            pltpu.VMEM((4, 4, 96, 128), BF16),
            pltpu.VMEM((4, 4, 96, 128), F32),
            pltpu.VMEM((4, 4, 96, 128), BF16),
            pltpu.VMEM((4, 4, 4, 24, 128), BF16),
            pltpu.VMEM((4, 16, 24, 128), BF16),
            pltpu.VMEM((2, 256, 768), BF16),
            pltpu.VMEM((2, 128, 128), BF16),
            pltpu.VMEM((2, 64, 2, 128), F32),
            pltpu.VMEM((64, 2, 128), F32),
            pltpu.VMEM((64, 2, 128), F32),
            pltpu.VMEM((64, 2, 128), F32),
            dma((11,)),
            dma((16,)), dma((16,)), dma((4, 4)), dma((16, 2)), dma((16, 2)),
            dma((4,)), dma((4,)), dma((4, 16)), dma((4, 16)), dma, dma, dma((64,)), dma((64,)),
        ],
        compiler_params=pltpu.CompilerParams(collective_id=0, has_side_effects=True),
        name="harmonic_sketch",
    )(*args)
    return jnp.transpose(result.reshape(4, 64))


def solution(mesh):
    return jax.shard_map(
        local,
        mesh=mesh,
        in_specs=(
            P("patch", "mode", None),
            P("patch", "mode"),
            P("patch", "mode", None, None),
            P("patch", "mode", None),
            P("mode", "patch"),
            P(),
            P("patch", "mode", None, None),
        ),
        out_specs=P(None, ("patch", "mode")),
        check_vma=False,
    )
```

```python
import functools
import math

import jax
import jax.numpy as jnp
import numpy as np
from jax import lax
from jax.experimental import pallas as pl
from jax.experimental.pallas import tpu as pltpu
from jax.sharding import PartitionSpec as P

F32 = jnp.float32
BF16 = jnp.bfloat16
MESH = pl.DeviceIdType.MESH
NM = 16


def fourier_tables():
    m1 = np.arange(64)[:, None]
    j1 = np.arange(64)[None, :]
    angle = 2.0 * math.pi * ((m1 * j1) % 64) / 64.0
    wa = np.concatenate([np.cos(angle), -np.sin(angle)], axis=0)
    low = np.arange(128)[:, None]
    j2 = np.arange(128)[None, :]
    turn = 2.0 * math.pi * (low * j2) / 8192.0
    wb = np.zeros((48, 2, 4, 4, 2, 64))
    g = np.arange(48)[:, None]
    fold = np.arange(64)[None, :]
    phi = 2.0 * math.pi * ((g * fold) % 64) / 64.0
    for dd in range(4):
        wb[:, 0, dd, dd, 0, :] = np.cos(phi)
        wb[:, 0, dd, dd, 1, :] = np.sin(phi)
        wb[:, 1, dd, dd, 0, :] = -np.sin(phi)
        wb[:, 1, dd, dd, 1, :] = np.cos(phi)
    return (
        jnp.asarray(wa.astype(np.float32), BF16),
        jnp.asarray(wb.reshape(384, 512).astype(np.float32), BF16),
        jnp.asarray(np.cos(turn), F32),
        jnp.asarray(np.sin(turn), F32),
    )


def iota2(shape, axis):
    return lax.broadcasted_iota(jnp.int32, shape, axis)


def onehot(test):
    return jnp.where(test, 1.0, 0.0).astype(BF16)


def dot(a, b):
    return jnp.dot(a, b, preferred_element_type=F32)


def dot_nt(a, b):
    return lax.dot_general(a, b, (((1,), (1,)), ((), ())), preferred_element_type=F32)


def kernel(
    sky_h, mask_h, noise_h, leg_h, band_h, cov_h, test_h, wa_h, wb_h, twc_h, tws_h,
    out,
    sky, mask, noise, leg, band, cov, test, wa, wb, twc, tws,
    bd, xsend, xrecv, xs, lown, lall, lf, four, alm_a, alm_b, pair, asend, arecv, tt, ce,
    ssend, srecv, fsend, frecv,
    in_sem, xs_sem, xr_sem, ls_sem, ld_sem, lf_sem, lr_sem, ps_sem, pr_sem,
    as_sem, ar_sem, ss_sem, sr_sem, fs_sem, fr_sem,
):
    p = lax.axis_index("patch")
    e = lax.axis_index("mode")
    core = lax.rem(p, 2)
    z = p // 2
    ex = e // 4
    ey = lax.rem(e, 4)

    def ahead(a, b):
        return lax.rem(ex + a, 4) * 4 + lax.rem(ey + b, 4)

    def behind(a, b):
        return lax.rem(ex + 4 - a, 4) * 4 + lax.rem(ey + 4 - b, 4)

    def plane(dz):
        return 2 * lax.rem(z + dz, 4) + core

    peers = [(dz, a, b) for dz in range(4) for a in range(4) for b in range(4) if dz + a + b > 0]
    peers.sort(key=lambda t: -sum(min(v, 4 - v) for v in t))

    barrier = pltpu.get_barrier_semaphore()
    pl.semaphore_signal(barrier, inc=1, device_id=(2 * z + 1 - core, e), device_id_type=MESH)
    greeted = [(dz, a, b) for dz, a, b in peers if dz == 0 or a + b == 0]
    for dz, a, b in greeted:
        pl.semaphore_signal(barrier, inc=1, device_id=(plane(dz), ahead(a, b)), device_id_type=MESH)

    hbm = (noise_h, sky_h, mask_h, leg_h, wa_h, twc_h, tws_h, wb_h, cov_h, band_h, test_h)
    vmem = (noise, sky, mask, leg, wa, twc, tws, wb, cov, band, test)
    loads = [pltpu.make_async_copy(a, b, in_sem.at[i]) for i, (a, b) in enumerate(zip(hbm, vmem))]
    for load in loads:
        load.start()

    row = iota2((512, 512), 0)
    lane = iota2((512, 512), 1)
    source = ((row >> 2) & 7) * 64 + (row >> 5) * 4 + (row & 3)
    order = onehot(lane == source)
    repeat = onehot((iota2((64, 512), 1) & 63) == iota2((64, 512), 0))
    loads[0].wait()
    moved = dot(order, noise[...].astype(BF16)).astype(BF16)
    wide = dot(moved, repeat)
    bd[...] = jnp.where((lane >> 6) == ((row >> 2) & 7), wide, 0.0).astype(BF16)
    loads[1].wait()
    loads[2].wait()
    for r in range(8):
        seen = jnp.broadcast_to(mask[r : r + 1, :].astype(F32), (64, 512)).astype(BF16)
        sky[64 * r : 64 * r + 64, :] = sky[64 * r : 64 * r + 64, :] * seen

    loads[3].wait()
    for h in range(2):
        for t in range(3):
            lown[h, t] = leg[32 * h : 32 * h + 32, 128 * t : 128 * t + 128].astype(BF16)

    def send_x(a, b):
        to = ahead(a, b)
        return pltpu.make_async_remote_copy(
            src_ref=xsend.at[to], dst_ref=xrecv.at[e], send_sem=xs_sem, recv_sem=xr_sem,
            device_id=(p, to), device_id_type=MESH)

    def send_l(a, b):
        return pltpu.make_async_remote_copy(
            src_ref=lown, dst_ref=lall.at[4 * a + b], send_sem=ls_sem, recv_sem=ld_sem.at[0 if a == 0 else 1],
            device_id=(p, ahead(a, b)), device_id_type=MESH)

    def relay_l(a, b, h):
        source, to = ((4 * a, ahead(0, b)), (b, ahead(a, 0)))[h]
        return pltpu.make_async_remote_copy(
            src_ref=lall.at[source, h], dst_ref=lall.at[4 * a + b, h],
            send_sem=lf_sem, recv_sem=lr_sem.at[a],
            device_id=(p, to), device_id_type=MESH)

    straight = [(0, 2), (2, 0), (0, 1), (0, 3), (1, 0), (3, 0)]

    pl.semaphore_wait(barrier, len(greeted) + 1)
    for a, b in straight:
        send_l(a, b).start()
    for n in range(4):
        q = lax.rem(ex + n, 4)
        white = dot(bd[pl.ds(pl.multiple_of(128 * q, 128), 128), :], sky[...]).astype(BF16)
        xsend[pl.ds(4 * q, 4)] = white.reshape(4, 32, 512)
        for b in range(4):
            if n + b > 0:
                send_x(n, b).start()

    loads[10].wait()
    loads[8].wait()
    split = onehot(iota2((256, 256), 1) == 2 * (iota2((256, 256), 0) & 127) + (iota2((256, 256), 0) >> 7))
    to = iota2((256, 512), 0)
    wanted = ((to >> 5) & 3) * 128 + (to >> 7) * 64 + ((to >> 1) & 15) * 4 + (to & 1) * 2
    columns = [onehot(iota2((256, 512), 1) == wanted + h) for h in range(2)]
    for b in range(3):
        block = dot(split, test[128 * b : 128 * b + 128].reshape(256, 512)).astype(BF16)
        for h in range(2):
            parts = dot_nt(columns[h], block).astype(BF16)
            tt[h, :, 128 * b : 128 * b + 128] = parts[:, :128]
            tt[h, :, 384 + 128 * b : 384 + 128 * b + 128] = parts[:, 128:]
    l128 = iota2((64, 128), 1)
    spread = onehot(iota2((64, 128), 0) == 4 * (l128 >> 3) + (l128 & 3))
    high = cov[...].astype(BF16)
    rest = (cov[...] - high.astype(F32)).astype(BF16)
    for n, piece in enumerate((high, rest)):
        wide_cov = dot(piece, spread)
        for t in range(2):
            ce[n, 64 * t : 64 * t + 64, :] = jnp.where(((l128 >> 2) & 1) == t, wide_cov, 0.0).astype(BF16)

    def copied(ref, sem):
        return pltpu.make_async_remote_copy(
            src_ref=ref, dst_ref=ref, send_sem=sem, recv_sem=sem, device_id=(p, e), device_id_type=MESH)

    def spread_x(ref, src):
        for h in range(4):
            xs[pl.ds(src * 4 + h, 32, stride=64), :] = ref[src, :, 128 * h : 128 * h + 128].astype(F32)

    def spread_l(ref, slot):
        for h in range(2):
            for t in range(3):
                lf[192 * slot + 64 * t + 32 * h : 192 * slot + 64 * t + 32 * h + 32, :] = ref[h, t].astype(F32)

    spread_x(xsend, e)
    spread_l(lown, 0)
    copied(lall.at[pl.ds(0, 3)], ld_sem.at[1]).wait_recv()
    for n in (1, 3, 2):
        for b in (2, 1, 3):
            relay_l(n, b, 0).start()
    copied(lall.at[pl.ds(0, 3)], ld_sem.at[0]).wait_recv()
    for n in (1, 3, 2):
        for a in (2, 1, 3):
            relay_l(a, n, 1).start()
    copied(xrecv.at[pl.ds(0, NM - 1)], xr_sem).wait_recv()

    def take_x(i, carry):
        spread_x(xrecv, lax.rem(e + i, NM))
        return carry

    lax.fori_loop(1, NM, take_x, 0)
    for a, b in straight:
        spread_l(lall.at[4 * a + b], 4 * a + b)

    loads[4].wait()
    loads[5].wait()
    loads[6].wait()
    loads[7].wait()
    left_half = iota2((64, 128), 1) < 64

    def transform(pair_index, carry):
        rows = []
        for s in range(2):
            base = pair_index * 512 + s * 256
            pix = [xs[pl.ds(pl.multiple_of(base + 64 * dd, 64), 64), :] for dd in range(4)]
            first = dot(wa[...], jnp.concatenate(pix, axis=1).astype(BF16))
            lanes = []
            for dd in range(4):
                re = first[:64, 128 * dd : 128 * dd + 128]
                im = first[64:, 128 * dd : 128 * dd + 128]
                halves = []
                for h in range(2):
                    c = twc[64 * h : 64 * h + 64, :]
                    sn = tws[64 * h : 64 * h + 64, :]
                    tr = re * c + im * sn
                    ti = im * c - re * sn
                    halves.append(
                        jnp.where(left_half, tr, ti) + pltpu.roll(jnp.where(left_half, ti, tr), 64, 1))
                lanes.append(jnp.concatenate(halves, axis=0).astype(BF16))
            rows.append(jnp.concatenate(lanes, axis=1))
        second = dot_nt(wb[...], jnp.concatenate(rows, axis=0))
        four[2 * pair_index] = second[:, :128]
        four[2 * pair_index + 1] = second[:, 128:]
        return carry

    lax.fori_loop(0, 4, transform, 0)

    def legendre(a, parity, put):
        def body(j, carry):
            acc = [[None, None] for _ in range(4)]
            for gi in range(2):
                q = 2 * j + gi
                b = q // 3
                g = 3 * (lax.rem(ex + 4 - a, 4) * 4 + lax.rem(ey + 4 - b, 4)) + q - 3 * b
                for r in range(8):
                    f = four[r, pl.ds(pl.multiple_of(g * 8, 8), 8), :]
                    for kk in range(4):
                        lrow = lf[pl.ds((12 * a + q) * 64 + r * 8 + 2 * kk + parity, 8, stride=0), :]
                        term = lrow * f
                        acc[kk][gi] = term if r == 0 else acc[kk][gi] + term
            for kk in range(4):
                put(kk, pl.ds(pl.multiple_of(j * 16, 16), 16), jnp.concatenate(acc[kk], axis=0))
            return carry

        lax.fori_loop(0, 6, body, 0)

    def to_core(n):
        return pltpu.make_async_remote_copy(
            src_ref=alm_a.at[n], dst_ref=pair.at[n], send_sem=ps_sem, recv_sem=pr_sem.at[n],
            device_id=(2 * z + 1 - core, e), device_id_type=MESH)

    def to_owner(dz, n, b):
        return pltpu.make_async_remote_copy(
            src_ref=asend.at[n, dz, b], dst_ref=arecv.at[16 * dz + e],
            send_sem=as_sem, recv_sem=ar_sem,
            device_id=(plane(dz), behind(n, b)), device_id_type=MESH)

    def group_terms(n):
        if n > 0:
            copied(lall.at[pl.ds(0, 3)], lr_sem.at[n]).wait_recv()
            for b in range(1, 4):
                spread_l(lall.at[4 * n + b], 4 * n + b)

        def put_a(kk, rows, value):
            alm_a[n, kk, rows, :] = value.astype(BF16)

        def put_b(kk, rows, value):
            alm_b[n, kk, rows, :] = value

        legendre(n, 1 - core, put_a)
        to_core(n).start()
        legendre(n, core, put_b)

    def group_pair(n):
        to_core(n).wait_recv()
        for dz in (2, 1, 3, 0):
            kk = lax.rem(z + dz, 4)
            both = (alm_b[n, kk] + pair[n, kk].astype(F32)).astype(BF16)
            for b in (2, 1, 3, 0):
                asend[n, dz, b] = both[24 * b : 24 * b + 24, :]
                if dz + n + b > 0:
                    to_owner(dz, n, b).start()

    for n in range(5):
        if n < 4:
            group_terms(n)
        if n > 0:
            group_pair(n - 1)
    arecv[e] = asend[0, 0, 0]
    copied(arecv.at[pl.ds(0, 63)], ar_sem).wait_recv()
    loads[9].wait()
    parts = sum(arecv[16 * dz : 16 * dz + 16].astype(F32) for dz in range(4))
    alm = jnp.concatenate(
        [parts[:, 8 * gl : 8 * gl + 8, :].reshape(128, 128) for gl in range(3)], axis=1).astype(BF16)
    mixed = dot(ce[0], alm) + dot(ce[1], alm)
    scaled = (mixed * band[...]).astype(BF16)
    scaled = jnp.concatenate([scaled[:64], scaled[64:]], axis=1)
    sketch = jnp.concatenate([dot_nt(tt[h], scaled) for h in range(2)], axis=1)
    ssend[...] = sketch.reshape(2, 64, 2, 128)

    to_sibling = pltpu.make_async_remote_copy(
        src_ref=ssend.at[1 - core], dst_ref=srecv, send_sem=ss_sem, recv_sem=sr_sem,
        device_id=(2 * z + 1 - core, e), device_id_type=MESH)
    to_sibling.start()
    to_sibling.wait_recv()
    fsend[...] = ssend[core] + srecv[...]

    def to_column(dz, a, b):
        column = lax.rem(z + dz, 4) * 16 + ahead(a, b)
        return pltpu.make_async_remote_copy(
            src_ref=fsend.at[column], dst_ref=frecv.at[16 * z + e],
            send_sem=fs_sem, recv_sem=fr_sem,
            device_id=(plane(dz), ahead(a, b)), device_id_type=MESH)

    for dz, a, b in peers:
        to_column(dz, a, b).start()
    frecv[16 * z + e] = fsend[16 * z + e]
    copied(frecv.at[pl.ds(0, 63)], fr_sem).wait_recv()
    out[...] = jnp.sum(frecv[...], axis=0)

    copied(xrecv.at[pl.ds(0, NM - 1)], xs_sem).wait_send()
    copied(lall.at[pl.ds(0, 6)], ls_sem).wait_send()
    copied(lall.at[pl.ds(0, 9)], lf_sem).wait_send()
    copied(alm_a, ps_sem).wait_send()
    copied(arecv.at[pl.ds(0, 63)], as_sem).wait_send()
    to_sibling.wait_send()
    copied(frecv.at[pl.ds(0, 63)], fs_sem).wait_send()


def local(sky_map, pixel_mask, noise_factor, cycle_legendre, band_power, channel_cov, test_matrix):
    wa, wb, twc, tws = fourier_tables()
    args = (
        jnp.transpose(sky_map, (0, 2, 1)).reshape(512, 512),
        pixel_mask,
        noise_factor.reshape(512, 64),
        jnp.transpose(cycle_legendre, (0, 2, 1)).reshape(64, 384),
        jnp.transpose(band_power),
        channel_cov,
        test_matrix.reshape(384, 2, 512),
        wa, wb, twc, tws,
    )
    dma = pltpu.SemaphoreType.DMA
    result = pl.pallas_call(
        kernel,
        out_shape=jax.ShapeDtypeStruct((2, 128), F32),
        in_specs=[pl.BlockSpec(memory_space=pl.ANY)] * len(args),
        out_specs=pl.BlockSpec(memory_space=pltpu.VMEM),
        scratch_shapes=[
            pltpu.VMEM((512, 512), BF16),
            pltpu.VMEM((8, 512), jnp.int32),
            pltpu.VMEM((512, 64), F32),
            pltpu.VMEM((64, 384), F32),
            pltpu.VMEM((1, 384), F32),
            pltpu.VMEM((64, 64), F32),
            pltpu.VMEM((384, 2, 512), BF16),
            pltpu.VMEM((128, 64), BF16),
            pltpu.VMEM((384, 512), BF16),
            pltpu.VMEM((128, 128), F32),
            pltpu.VMEM((128, 128), F32),
            pltpu.VMEM((512, 512), BF16),
            pltpu.VMEM((16, 32, 512), BF16),
            pltpu.VMEM((16, 32, 512), BF16),
            pltpu.VMEM((2048, 128), F32),
            pltpu.VMEM((2, 3, 32, 128), BF16),
            pltpu.VMEM((16, 2, 3, 32, 128), BF16),
            pltpu.VMEM((3072, 128), F32),
            pltpu.VMEM((8, 384, 128), F32),
            pltpu.VMEM((4, 4, 96, 128), BF16),
            pltpu.VMEM((4, 4, 96, 128), F32),
            pltpu.VMEM((4, 4, 96, 128), BF16),
            pltpu.VMEM((4, 4, 4, 24, 128), BF16),
            pltpu.VMEM((64, 24, 128), BF16),
            pltpu.VMEM((2, 256, 768), BF16),
            pltpu.VMEM((2, 128, 128), BF16),
            pltpu.VMEM((2, 64, 2, 128), F32),
            pltpu.VMEM((64, 2, 128), F32),
            pltpu.VMEM((64, 2, 128), F32),
            pltpu.VMEM((64, 2, 128), F32),
            dma((11,)), dma, dma, dma, dma((2,)), dma, dma((4,)),
            dma, dma((4,)), dma, dma, dma, dma, dma, dma,
        ],
        compiler_params=pltpu.CompilerParams(collective_id=0, has_side_effects=True),
        name="harmonic_sketch",
    )(*args)
    return jnp.transpose(result.reshape(4, 64))


def solution(mesh):
    return jax.shard_map(
        local,
        mesh=mesh,
        in_specs=(
            P("patch", "mode", None),
            P("patch", "mode"),
            P("patch", "mode", None, None),
            P("patch", "mode", None),
            P("mode", "patch"),
            P(),
            P("patch", "mode", None, None),
        ),
        out_specs=P(None, ("patch", "mode")),
        check_vma=False,
    )
```

```python
import functools
import math

import jax
import jax.numpy as jnp
import numpy as np
from jax import lax
from jax.experimental import pallas as pl
from jax.experimental.pallas import tpu as pltpu
from jax.sharding import PartitionSpec as P

F32 = jnp.float32
BF16 = jnp.bfloat16
MESH = pl.DeviceIdType.MESH
NM = 16


def fourier_tables():
    m1 = np.arange(64)[:, None]
    j1 = np.arange(64)[None, :]
    angle = 2.0 * math.pi * ((m1 * j1) % 64) / 64.0
    wa = np.concatenate([np.cos(angle), -np.sin(angle)], axis=0)
    low = np.arange(128)[:, None]
    j2 = np.arange(128)[None, :]
    turn = 2.0 * math.pi * (low * j2) / 8192.0
    g = np.arange(48)[:, None]
    phi = 2.0 * math.pi * ((g * j2) % 64) / 64.0
    wb = np.zeros((48, 2, 2, 128))
    wb[:, 0, 0, :] = np.cos(phi)
    wb[:, 0, 1, :] = np.sin(phi)
    wb[:, 1, 0, :] = -np.sin(phi)
    wb[:, 1, 1, :] = np.cos(phi)
    return (
        jnp.asarray(wa.astype(np.float32), BF16),
        jnp.asarray(wb.reshape(96, 256).astype(np.float32), BF16),
        jnp.asarray(np.cos(turn), F32),
        jnp.asarray(np.sin(turn), F32),
    )


def iota2(shape, axis):
    return lax.broadcasted_iota(jnp.int32, shape, axis)


def onehot(test):
    return jnp.where(test, 1.0, 0.0).astype(BF16)


def dot(a, b):
    return jnp.dot(a, b, preferred_element_type=F32)


def dot_nt(a, b):
    return lax.dot_general(a, b, (((1,), (1,)), ((), ())), preferred_element_type=F32)


def kernel(
    sky_h, mask_h, noise_h, leg_h, band_h, cov_h, test_h, wa_h, wb_h, twc_h, tws_h,
    out,
    sky, mask, noise, leg, band, cov, test, wa, wb, twc, tws,
    bd, xsend, xrecv, xs, fa, turned, lown, lall, lf, four, alm_a, alm_b, pair, asend, arecv, tt, ce,
    ssend, srecv, fsend, frecv,
    in_sem, xs_sem, xr_sem, ls_sem, ld_sem, lf_sem, lr_sem, ps_sem, pr_sem,
    as_sem, ar_sem, ss_sem, sr_sem, fs_sem, fr_sem,
):
    p = lax.axis_index("patch")
    e = lax.axis_index("mode")
    core = lax.rem(p, 2)
    z = p // 2
    ex = e // 4
    ey = lax.rem(e, 4)

    def ahead(a, b):
        return lax.rem(ex + a, 4) * 4 + lax.rem(ey + b, 4)

    def behind(a, b):
        return lax.rem(ex + 4 - a, 4) * 4 + lax.rem(ey + 4 - b, 4)

    def plane(dz):
        return 2 * lax.rem(z + dz, 4) + core

    peers = [(dz, a, b) for dz in range(4) for a in range(4) for b in range(4) if dz + a + b > 0]
    peers.sort(key=lambda t: -sum(min(v, 4 - v) for v in t))

    barrier = pltpu.get_barrier_semaphore()
    pl.semaphore_signal(barrier, inc=1, device_id=(2 * z + 1 - core, e), device_id_type=MESH)
    greeted = [(dz, a, b) for dz, a, b in peers if dz == 0 or a + b == 0]
    for dz, a, b in greeted:
        pl.semaphore_signal(barrier, inc=1, device_id=(plane(dz), ahead(a, b)), device_id_type=MESH)

    hbm = (noise_h, sky_h, mask_h, leg_h, wa_h, twc_h, tws_h, wb_h, cov_h, band_h, test_h)
    vmem = (noise, sky, mask, leg, wa, twc, tws, wb, cov, band, test)
    loads = [pltpu.make_async_copy(a, b, in_sem.at[i]) for i, (a, b) in enumerate(zip(hbm, vmem))]
    for load in loads:
        load.start()

    row = iota2((512, 512), 0)
    lane = iota2((512, 512), 1)
    source = ((row >> 2) & 7) * 64 + (row >> 5) * 4 + (row & 3)
    order = onehot(lane == source)
    repeat = onehot((iota2((64, 512), 1) & 63) == iota2((64, 512), 0))
    loads[0].wait()
    moved = dot(order, noise[...].astype(BF16)).astype(BF16)
    wide = dot(moved, repeat)
    bd[...] = jnp.where((lane >> 6) == ((row >> 2) & 7), wide, 0.0).astype(BF16)
    loads[1].wait()
    loads[2].wait()
    for r in range(8):
        seen = jnp.broadcast_to(mask[r : r + 1, :].astype(F32), (64, 512)).astype(BF16)
        sky[64 * r : 64 * r + 64, :] = sky[64 * r : 64 * r + 64, :] * seen

    loads[3].wait()
    for h in range(2):
        for t in range(3):
            lown[h, t] = leg[32 * h : 32 * h + 32, 128 * t : 128 * t + 128].astype(BF16)

    def send_x(a, b, half):
        to = ahead(a, b)
        return pltpu.make_async_remote_copy(
            src_ref=xsend.at[half, to], dst_ref=xrecv.at[half, e], send_sem=xs_sem, recv_sem=xr_sem.at[half],
            device_id=(p, to), device_id_type=MESH)

    def send_l(a, b):
        return pltpu.make_async_remote_copy(
            src_ref=lown, dst_ref=lall.at[4 * a + b], send_sem=ls_sem, recv_sem=ld_sem.at[0 if a == 0 else 1],
            device_id=(p, ahead(a, b)), device_id_type=MESH)

    def relay_l(a, b, h):
        source, to = ((4 * a, ahead(0, b)), (b, ahead(a, 0)))[h]
        return pltpu.make_async_remote_copy(
            src_ref=lall.at[source, h], dst_ref=lall.at[4 * a + b, h],
            send_sem=lf_sem, recv_sem=lr_sem.at[a],
            device_id=(p, to), device_id_type=MESH)

    straight = [(0, 2), (2, 0), (0, 1), (0, 3), (1, 0), (3, 0)]

    pl.semaphore_wait(barrier, len(greeted) + 1)
    for a, b in straight:
        send_l(a, b).start()
    for n in range(4):
        q = lax.rem(ex + n, 4)
        white = dot(bd[pl.ds(pl.multiple_of(128 * q, 128), 128), :], sky[...]).astype(BF16)
        white = white.reshape(4, 32, 512)
        for half in range(2):
            xsend[half, pl.ds(4 * q, 4)] = white[:, 16 * half : 16 * half + 16, :]
        for b in range(4):
            if n + b > 0:
                send_x(n, b, 0).start()
    for a in range(4):
        for b in range(4):
            if a + b > 0:
                send_x(a, b, 1).start()

    loads[10].wait()
    loads[8].wait()
    split = onehot(iota2((256, 256), 1) == 2 * (iota2((256, 256), 0) & 127) + (iota2((256, 256), 0) >> 7))
    to = iota2((256, 512), 0)
    wanted = ((to >> 5) & 3) * 128 + (to >> 7) * 64 + ((to >> 1) & 15) * 4 + (to & 1) * 2
    columns = [onehot(iota2((256, 512), 1) == wanted + h) for h in range(2)]
    for b in range(3):
        block = dot(split, test[128 * b : 128 * b + 128].reshape(256, 512)).astype(BF16)
        for h in range(2):
            parts = dot_nt(columns[h], block).astype(BF16)
            tt[h, :, 128 * b : 128 * b + 128] = parts[:, :128]
            tt[h, :, 384 + 128 * b : 384 + 128 * b + 128] = parts[:, 128:]
    l128 = iota2((64, 128), 1)
    spread = onehot(iota2((64, 128), 0) == 4 * (l128 >> 3) + (l128 & 3))
    high = cov[...].astype(BF16)
    rest = (cov[...] - high.astype(F32)).astype(BF16)
    for n, piece in enumerate((high, rest)):
        wide_cov = dot(piece, spread)
        for t in range(2):
            ce[n, 64 * t : 64 * t + 64, :] = jnp.where(((l128 >> 2) & 1) == t, wide_cov, 0.0).astype(BF16)

    def copied(ref, sem):
        return pltpu.make_async_remote_copy(
            src_ref=ref, dst_ref=ref, send_sem=sem, recv_sem=sem, device_id=(p, e), device_id_type=MESH)

    def spread_x(ref, half, src):
        for h in range(4):
            xs[pl.ds(1024 * half + src * 4 + h, 16, stride=64), :] = (
                ref[half, src, :, 128 * h : 128 * h + 128].astype(F32))

    def spread_l(ref, slot):
        for h in range(2):
            for t in range(3):
                lf[192 * slot + 64 * t + 32 * h : 192 * slot + 64 * t + 32 * h + 32, :] = ref[h, t].astype(F32)

    spread_x(xsend, 0, e)
    spread_x(xsend, 1, e)
    spread_l(lown, 0)
    copied(lall.at[pl.ds(0, 3)], ld_sem.at[1]).wait_recv()
    for n in (1, 3, 2):
        for b in (2, 1, 3):
            relay_l(n, b, 0).start()
    copied(lall.at[pl.ds(0, 3)], ld_sem.at[0]).wait_recv()
    for n in (1, 3, 2):
        for a in (2, 1, 3):
            relay_l(a, n, 1).start()
    for a, b in straight:
        spread_l(lall.at[4 * a + b], 4 * a + b)
    for n in (4, 5, 6, 7):
        loads[n].wait()

    def twiddle(r, carry):
        for h in range(2):
            c = twc[64 * h : 64 * h + 64, :]
            sn = tws[64 * h : 64 * h + 64, :]
            rows = pl.ds(pl.multiple_of(lax.rem(r, 2) * 128 + 64 * h, 64), 64)
            for dd in range(4):
                cols = slice(128 * dd, 128 * dd + 128)
                re = fa[pl.ds(pl.multiple_of(128 * r, 128), 64), cols]
                im = fa[pl.ds(pl.multiple_of(128 * r + 64, 64), 64), cols]
                unit = 4 * (r // 2) + dd
                turned[unit, rows, 0:128] = (re * c + im * sn).astype(BF16)
                turned[unit, rows, 128:256] = (im * c - re * sn).astype(BF16)
        return carry

    for half in range(2):
        copied(xrecv.at[half, pl.ds(0, NM - 1)], xr_sem.at[half]).wait_recv()

        def take_x(i, carry, half=half):
            spread_x(xrecv, half, lax.rem(e + i, NM))
            return carry

        lax.fori_loop(1, NM, take_x, 0)
        for r in range(4 * half, 4 * half + 4):
            pix = jnp.concatenate([xs[256 * r + 64 * dd : 256 * r + 64 * dd + 64, :] for dd in range(4)], axis=1)
            fa[128 * r : 128 * r + 128, :] = dot(wa[...], pix.astype(BF16))
        lax.fori_loop(4 * half, 4 * half + 4, twiddle, 0)
        for unit in range(8 * half, 8 * half + 8):
            second = dot_nt(wb[...], turned[unit])
            for s in range(2):
                start = (2 * (unit // 4) + s) * 384 + unit % 4
                four[pl.ds(start, 96, stride=4), :] = second[:, 128 * s : 128 * s + 128]

    def legendre(a, parity, put):
        def body(j, carry):
            acc = [[None, None] for _ in range(4)]
            for gi in range(2):
                q = 2 * j + gi
                b = q // 3
                g = 3 * (lax.rem(ex + 4 - a, 4) * 4 + lax.rem(ey + 4 - b, 4)) + q - 3 * b
                for r in range(8):
                    f = four[pl.ds(pl.multiple_of(r * 384 + g * 8, 8), 8), :]
                    for kk in range(4):
                        lrow = lf[pl.ds((12 * a + q) * 64 + r * 8 + 2 * kk + parity, 8, stride=0), :]
                        term = lrow * f
                        acc[kk][gi] = term if r == 0 else acc[kk][gi] + term
            for kk in range(4):
                put(kk, pl.ds(pl.multiple_of(j * 16, 16), 16), jnp.concatenate(acc[kk], axis=0))
            return carry

        lax.fori_loop(0, 6, body, 0, unroll=3)

    def to_core(n):
        return pltpu.make_async_remote_copy(
            src_ref=alm_a.at[n], dst_ref=pair.at[n], send_sem=ps_sem, recv_sem=pr_sem.at[n],
            device_id=(2 * z + 1 - core, e), device_id_type=MESH)

    def to_owner(dz, n, b):
        return pltpu.make_async_remote_copy(
            src_ref=asend.at[n, dz, b], dst_ref=arecv.at[16 * dz + e],
            send_sem=as_sem, recv_sem=ar_sem,
            device_id=(plane(dz), behind(n, b)), device_id_type=MESH)

    def group_terms(n):
        if n > 0:
            copied(lall.at[pl.ds(0, 3)], lr_sem.at[n]).wait_recv()
            for b in range(1, 4):
                spread_l(lall.at[4 * n + b], 4 * n + b)

        def put_a(kk, rows, value):
            alm_a[n, kk, rows, :] = value.astype(BF16)

        def put_b(kk, rows, value):
            alm_b[n, kk, rows, :] = value

        legendre(n, 1 - core, put_a)
        to_core(n).start()
        legendre(n, core, put_b)

    def group_pair(n):
        to_core(n).wait_recv()
        for dz in (2, 1, 3, 0):
            kk = lax.rem(z + dz, 4)
            both = (alm_b[n, kk] + pair[n, kk].astype(F32)).astype(BF16)
            for b in (2, 1, 3, 0):
                asend[n, dz, b] = both[24 * b : 24 * b + 24, :]
                if dz + n + b > 0:
                    to_owner(dz, n, b).start()

    for n in range(5):
        if n < 4:
            group_terms(n)
        if n > 0:
            group_pair(n - 1)
    arecv[e] = asend[0, 0, 0]
    copied(arecv.at[pl.ds(0, 63)], ar_sem).wait_recv()
    loads[9].wait()
    parts = sum(arecv[16 * dz : 16 * dz + 16].astype(F32) for dz in range(4))
    alm = jnp.concatenate(
        [parts[:, 8 * gl : 8 * gl + 8, :].reshape(128, 128) for gl in range(3)], axis=1).astype(BF16)
    mixed = dot(ce[0], alm) + dot(ce[1], alm)
    scaled = (mixed * band[...]).astype(BF16)
    scaled = jnp.concatenate([scaled[:64], scaled[64:]], axis=1)
    sketch = jnp.concatenate([dot_nt(tt[h], scaled) for h in range(2)], axis=1)
    ssend[...] = sketch.reshape(2, 64, 2, 128)

    to_sibling = pltpu.make_async_remote_copy(
        src_ref=ssend.at[1 - core], dst_ref=srecv, send_sem=ss_sem, recv_sem=sr_sem,
        device_id=(2 * z + 1 - core, e), device_id_type=MESH)
    to_sibling.start()
    to_sibling.wait_recv()
    fsend[...] = ssend[core] + srecv[...]

    def to_column(dz, a, b):
        column = lax.rem(z + dz, 4) * 16 + ahead(a, b)
        return pltpu.make_async_remote_copy(
            src_ref=fsend.at[column], dst_ref=frecv.at[16 * z + e],
            send_sem=fs_sem, recv_sem=fr_sem,
            device_id=(plane(dz), ahead(a, b)), device_id_type=MESH)

    for dz, a, b in peers:
        to_column(dz, a, b).start()
    frecv[16 * z + e] = fsend[16 * z + e]
    copied(frecv.at[pl.ds(0, 63)], fr_sem).wait_recv()
    out[...] = jnp.sum(frecv[...], axis=0)

    copied(xrecv.at[:, pl.ds(0, NM - 1)], xs_sem).wait_send()
    copied(lall.at[pl.ds(0, 6)], ls_sem).wait_send()
    copied(lall.at[pl.ds(0, 9)], lf_sem).wait_send()
    copied(alm_a, ps_sem).wait_send()
    copied(arecv.at[pl.ds(0, 63)], as_sem).wait_send()
    to_sibling.wait_send()
    copied(frecv.at[pl.ds(0, 63)], fs_sem).wait_send()


def local(sky_map, pixel_mask, noise_factor, cycle_legendre, band_power, channel_cov, test_matrix):
    wa, wb, twc, tws = fourier_tables()
    args = (
        jnp.transpose(sky_map, (0, 2, 1)).reshape(512, 512),
        pixel_mask,
        noise_factor.reshape(512, 64),
        jnp.transpose(cycle_legendre, (0, 2, 1)).reshape(64, 384),
        jnp.transpose(band_power),
        channel_cov,
        test_matrix.reshape(384, 2, 512),
        wa, wb, twc, tws,
    )
    dma = pltpu.SemaphoreType.DMA
    result = pl.pallas_call(
        kernel,
        out_shape=jax.ShapeDtypeStruct((2, 128), F32),
        in_specs=[pl.BlockSpec(memory_space=pl.ANY)] * len(args),
        out_specs=pl.BlockSpec(memory_space=pltpu.VMEM),
        scratch_shapes=[
            pltpu.VMEM((512, 512), BF16),
            pltpu.VMEM((8, 512), jnp.int32),
            pltpu.VMEM((512, 64), F32),
            pltpu.VMEM((64, 384), F32),
            pltpu.VMEM((1, 384), F32),
            pltpu.VMEM((64, 64), F32),
            pltpu.VMEM((384, 2, 512), BF16),
            pltpu.VMEM((128, 64), BF16),
            pltpu.VMEM((96, 256), BF16),
            pltpu.VMEM((128, 128), F32),
            pltpu.VMEM((128, 128), F32),
            pltpu.VMEM((512, 512), BF16),
            pltpu.VMEM((2, 16, 16, 512), BF16),
            pltpu.VMEM((2, 16, 16, 512), BF16),
            pltpu.VMEM((2048, 128), F32),
            pltpu.VMEM((1024, 512), F32),
            pltpu.VMEM((16, 256, 256), BF16),
            pltpu.VMEM((2, 3, 32, 128), BF16),
            pltpu.VMEM((16, 2, 3, 32, 128), BF16),
            pltpu.VMEM((3072, 128), F32),
            pltpu.VMEM((3072, 128), F32),
            pltpu.VMEM((4, 4, 96, 128), BF16),
            pltpu.VMEM((4, 4, 96, 128), F32),
            pltpu.VMEM((4, 4, 96, 128), BF16),
            pltpu.VMEM((4, 4, 4, 24, 128), BF16),
            pltpu.VMEM((64, 24, 128), BF16),
            pltpu.VMEM((2, 256, 768), BF16),
            pltpu.VMEM((2, 128, 128), BF16),
            pltpu.VMEM((2, 64, 2, 128), F32),
            pltpu.VMEM((64, 2, 128), F32),
            pltpu.VMEM((64, 2, 128), F32),
            pltpu.VMEM((64, 2, 128), F32),
            dma((11,)), dma, dma((2,)), dma, dma((2,)), dma, dma((4,)),
            dma, dma((4,)), dma, dma, dma, dma, dma, dma,
        ],
        compiler_params=pltpu.CompilerParams(collective_id=0, has_side_effects=True),
        name="harmonic_sketch",
    )(*args)
    return jnp.transpose(result.reshape(4, 64))


def solution(mesh):
    return jax.shard_map(
        local,
        mesh=mesh,
        in_specs=(
            P("patch", "mode", None),
            P("patch", "mode"),
            P("patch", "mode", None, None),
            P("patch", "mode", None),
            P("mode", "patch"),
            P(),
            P("patch", "mode", None, None),
        ),
        out_specs=P(None, ("patch", "mode")),
        check_vma=False,
    )
```

```python
import functools
import math

import jax
import jax.numpy as jnp
import numpy as np
from jax import lax
from jax.experimental import pallas as pl
from jax.experimental.pallas import tpu as pltpu
from jax.sharding import PartitionSpec as P

F32 = jnp.float32
BF16 = jnp.bfloat16
MESH = pl.DeviceIdType.MESH
NM = 16


def fourier_tables():
    m1 = np.arange(64)[:, None]
    j1 = np.arange(64)[None, :]
    angle = 2.0 * math.pi * ((m1 * j1) % 64) / 64.0
    wa = np.concatenate([np.cos(angle), -np.sin(angle)], axis=0)
    low = np.arange(128)[:, None]
    j2 = np.arange(128)[None, :]
    turn = 2.0 * math.pi * (low * j2) / 8192.0
    g = np.arange(48)[:, None]
    phi = 2.0 * math.pi * ((g * j2) % 64) / 64.0
    wb = np.zeros((48, 2, 2, 128))
    wb[:, 0, 0, :] = np.cos(phi)
    wb[:, 0, 1, :] = np.sin(phi)
    wb[:, 1, 0, :] = -np.sin(phi)
    wb[:, 1, 1, :] = np.cos(phi)
    return (
        jnp.asarray(wa.astype(np.float32), BF16),
        jnp.asarray(wb.reshape(96, 256).astype(np.float32), BF16),
        jnp.asarray(np.cos(turn), F32),
        jnp.asarray(np.sin(turn), F32),
    )


def iota2(shape, axis):
    return lax.broadcasted_iota(jnp.int32, shape, axis)


def onehot(test):
    return jnp.where(test, 1.0, 0.0).astype(BF16)


def dot(a, b):
    return jnp.dot(a, b, preferred_element_type=F32)


def dot_nt(a, b):
    return lax.dot_general(a, b, (((1,), (1,)), ((), ())), preferred_element_type=F32)


def kernel(
    sky_h, mask_h, noise_h, leg_h, band_h, cov_h, test_h, wa_h, wb_h, twc_h, tws_h,
    out,
    sky, mask, noise, leg, band, cov, test, wa, wb, twc, tws,
    bd, xsend, xrecv, xs, fa, turned, lown, lall, lf, four, alm_a, alm_b, pair, asend, arecv, tt, ce,
    ssend, srecv, fsend, frecv,
    in_sem, xs_sem, xr_sem, ls_sem, ld_sem, lf_sem, lr_sem, ps_sem, pr_sem,
    as_sem, ar_sem, ss_sem, sr_sem, fs_sem, fr_sem,
):
    p = lax.axis_index("patch")
    e = lax.axis_index("mode")
    core = lax.rem(p, 2)
    z = p // 2
    ex = e // 4
    ey = lax.rem(e, 4)

    def ahead(a, b):
        return lax.rem(ex + a, 4) * 4 + lax.rem(ey + b, 4)

    def behind(a, b):
        return lax.rem(ex + 4 - a, 4) * 4 + lax.rem(ey + 4 - b, 4)

    def plane(dz):
        return 2 * lax.rem(z + dz, 4) + core

    peers = [(dz, a, b) for dz in range(4) for a in range(4) for b in range(4) if dz + a + b > 0]
    peers.sort(key=lambda t: -sum(min(v, 4 - v) for v in t))

    barrier = pltpu.get_barrier_semaphore()
    pl.semaphore_signal(barrier, inc=1, device_id=(2 * z + 1 - core, e), device_id_type=MESH)
    greeted = [(dz, a, b) for dz, a, b in peers if dz == 0 or a + b == 0]
    for dz, a, b in greeted:
        pl.semaphore_signal(barrier, inc=1, device_id=(plane(dz), ahead(a, b)), device_id_type=MESH)

    hbm = (noise_h, sky_h, mask_h, leg_h, wa_h, twc_h, tws_h, wb_h, cov_h, band_h, test_h)
    vmem = (noise, sky, mask, leg, wa, twc, tws, wb, cov, band, test)
    loads = [pltpu.make_async_copy(a, b, in_sem.at[i]) for i, (a, b) in enumerate(zip(hbm, vmem))]
    for load in loads:
        load.start()

    row = iota2((512, 512), 0)
    lane = iota2((512, 512), 1)
    source = ((row >> 2) & 7) * 64 + (row >> 5) * 4 + (row & 3)
    order = onehot(lane == source)
    repeat = onehot((iota2((64, 512), 1) & 63) == iota2((64, 512), 0))
    loads[0].wait()
    moved = dot(order, noise[...].astype(BF16)).astype(BF16)
    wide = dot(moved, repeat)
    bd[...] = jnp.where((lane >> 6) == ((row >> 2) & 7), wide, 0.0).astype(BF16)
    loads[1].wait()
    loads[2].wait()
    for r in range(8):
        seen = jnp.broadcast_to(mask[r : r + 1, :].astype(F32), (64, 512)).astype(BF16)
        sky[64 * r : 64 * r + 64, :] = sky[64 * r : 64 * r + 64, :] * seen

    loads[3].wait()
    for h in range(2):
        for t in range(3):
            lown[h, t] = leg[32 * h : 32 * h + 32, 128 * t : 128 * t + 128].astype(BF16)

    def send_x(a, b, half):
        to = ahead(a, b)
        return pltpu.make_async_remote_copy(
            src_ref=xsend.at[half, to], dst_ref=xrecv.at[half, e], send_sem=xs_sem, recv_sem=xr_sem.at[half],
            device_id=(p, to), device_id_type=MESH)

    def send_l(a, b):
        return pltpu.make_async_remote_copy(
            src_ref=lown, dst_ref=lall.at[4 * a + b], send_sem=ls_sem, recv_sem=ld_sem.at[0 if a == 0 else 1],
            device_id=(p, ahead(a, b)), device_id_type=MESH)

    def relay_l(a, b, h):
        source, to = ((4 * a, ahead(0, b)), (b, ahead(a, 0)))[h]
        return pltpu.make_async_remote_copy(
            src_ref=lall.at[source, h], dst_ref=lall.at[4 * a + b, h],
            send_sem=lf_sem, recv_sem=lr_sem.at[(b - a) % 3],
            device_id=(p, to), device_id_type=MESH)

    shifts = [(a, (a + n) % 4) for n in range(4) for a in range(4)]
    order = [(0, 0), (0, 2), (0, 1), (0, 3), (2, 0), (1, 0), (3, 0)]
    order += [(a, (a + n - 1) % 3 + 1) for n in range(3) for a in range(1, 4)]
    groups = [(0, 4), (4, 7), (7, 10), (10, 13), (13, 16)]
    straight = [(0, 2), (2, 0), (0, 1), (0, 3), (1, 0), (3, 0)]

    pl.semaphore_wait(barrier, len(greeted) + 1)
    for q in range(4):
        white = dot(bd[128 * q : 128 * q + 128, :], sky[...]).astype(BF16).reshape(4, 32, 512)
        for half in range(2):
            xsend[half, 4 * q : 4 * q + 4] = white[:, 16 * half : 16 * half + 16, :]
    for half in range(2):
        for a, b in shifts:
            if a + b > 0:
                send_x(a, b, half).start()
        if half == 0:
            for a, b in straight:
                send_l(a, b).start()

    loads[10].wait()
    loads[8].wait()
    split = onehot(iota2((256, 256), 1) == 2 * (iota2((256, 256), 0) & 127) + (iota2((256, 256), 0) >> 7))
    to = iota2((256, 512), 0)
    wanted = ((to >> 5) & 3) * 128 + (to >> 7) * 64 + ((to >> 1) & 15) * 4 + (to & 1) * 2
    columns = [onehot(iota2((256, 512), 1) == wanted + h) for h in range(2)]
    for b in range(3):
        block = dot(split, test[128 * b : 128 * b + 128].reshape(256, 512)).astype(BF16)
        for h in range(2):
            parts = dot_nt(columns[h], block).astype(BF16)
            tt[h, :, 128 * b : 128 * b + 128] = parts[:, :128]
            tt[h, :, 384 + 128 * b : 384 + 128 * b + 128] = parts[:, 128:]
    l128 = iota2((64, 128), 1)
    spread = onehot(iota2((64, 128), 0) == 4 * (l128 >> 3) + (l128 & 3))
    high = cov[...].astype(BF16)
    rest = (cov[...] - high.astype(F32)).astype(BF16)
    for n, piece in enumerate((high, rest)):
        wide_cov = dot(piece, spread)
        for t in range(2):
            ce[n, 64 * t : 64 * t + 64, :] = jnp.where(((l128 >> 2) & 1) == t, wide_cov, 0.0).astype(BF16)

    def copied(ref, sem):
        return pltpu.make_async_remote_copy(
            src_ref=ref, dst_ref=ref, send_sem=sem, recv_sem=sem, device_id=(p, e), device_id_type=MESH)

    def spread_x(ref, half, src):
        for h in range(4):
            xs[pl.ds(1024 * half + src * 4 + h, 16, stride=64), :] = (
                ref[half, src, :, 128 * h : 128 * h + 128].astype(F32))

    def spread_l(ref, place):
        for h in range(2):
            for t in range(3):
                lf[192 * place + 64 * t + 32 * h : 192 * place + 64 * t + 32 * h + 32, :] = ref[h, t].astype(F32)

    spread_x(xsend, 0, e)
    spread_x(xsend, 1, e)
    spread_l(lown, 0)
    for n in (4, 5, 6, 7):
        loads[n].wait()

    def twiddle(r, carry):
        for h in range(2):
            c = twc[64 * h : 64 * h + 64, :]
            sn = tws[64 * h : 64 * h + 64, :]
            rows = pl.ds(pl.multiple_of(lax.rem(r, 2) * 128 + 64 * h, 64), 64)
            for dd in range(4):
                cols = slice(128 * dd, 128 * dd + 128)
                re = fa[pl.ds(pl.multiple_of(128 * r, 128), 64), cols]
                im = fa[pl.ds(pl.multiple_of(128 * r + 64, 64), 64), cols]
                unit = 4 * (r // 2) + dd
                turned[unit, rows, 0:128] = (re * c + im * sn).astype(BF16)
                turned[unit, rows, 128:256] = (im * c - re * sn).astype(BF16)
        return carry

    for half in range(2):
        copied(xrecv.at[half, pl.ds(0, NM - 1)], xr_sem.at[half]).wait_recv()

        def take_x(i, carry, half=half):
            spread_x(xrecv, half, lax.rem(e + i, NM))
            return carry

        lax.fori_loop(1, NM, take_x, 0)
        for r in range(4 * half, 4 * half + 4):
            pix = jnp.concatenate([xs[256 * r + 64 * dd : 256 * r + 64 * dd + 64, :] for dd in range(4)], axis=1)
            fa[128 * r : 128 * r + 128, :] = dot(wa[...], pix.astype(BF16))
        lax.fori_loop(4 * half, 4 * half + 4, twiddle, 0)
        for unit in range(8 * half, 8 * half + 8):
            second = dot_nt(wb[...], turned[unit])
            for s in range(2):
                start = (2 * (unit // 4) + s) * 384 + unit % 4
                four[pl.ds(start, 96, stride=4), :] = second[:, 128 * s : 128 * s + 128]
        if half == 0:
            copied(lall.at[pl.ds(0, 3)], ld_sem.at[1]).wait_recv()
            copied(lall.at[pl.ds(0, 3)], ld_sem.at[0]).wait_recv()
            for n in (1, 3, 2):
                for m in (2, 1, 3):
                    relay_l(n, m, 0).start()
                    relay_l(m, n, 1).start()
            for place in range(1, 7):
                a, b = order[place]
                spread_l(lall.at[4 * a + b], place)

    def legendre(place, parity, put):
        a, b = order[place]
        owner = behind(a, b)
        for kk0 in range(0, 4, 2):
            acc = [[None] * 3 for _ in range(2)]
            for gl in range(3):
                for r in range(8):
                    f = four[pl.ds(pl.multiple_of(384 * r + 24 * owner + 8 * gl, 8), 8), :]
                    for kk in range(2):
                        lrow = lf[pl.ds(192 * place + 64 * gl + 8 * r + 2 * (kk0 + kk) + parity, 8, stride=0), :]
                        term = lrow * f
                        acc[kk][gl] = term if r == 0 else acc[kk][gl] + term
            for kk in range(2):
                put(kk0 + kk, jnp.concatenate(acc[kk], axis=0))

    def to_core(n):
        first, last = groups[n]
        part = pl.ds(first, last - first)
        return pltpu.make_async_remote_copy(
            src_ref=alm_a.at[part], dst_ref=pair.at[part], send_sem=ps_sem, recv_sem=pr_sem.at[n],
            device_id=(2 * z + 1 - core, e), device_id_type=MESH)

    def to_owner(dz, place):
        a, b = order[place]
        return pltpu.make_async_remote_copy(
            src_ref=asend.at[place, dz], dst_ref=arecv.at[16 * dz + e],
            send_sem=as_sem, recv_sem=ar_sem,
            device_id=(plane(dz), behind(a, b)), device_id_type=MESH)

    def group_terms(n):
        if n >= 2:
            copied(lall.at[pl.ds(0, 3)], lr_sem.at[n - 2]).wait_recv()
            for place in range(*groups[n]):
                a, b = order[place]
                spread_l(lall.at[4 * a + b], place)

        for place in range(*groups[n]):
            def put_a(kk, value):
                alm_a[place, kk] = value.astype(BF16)

            legendre(place, 1 - core, put_a)
        to_core(n).start()
        for place in range(*groups[n]):
            def put_b(kk, value):
                alm_b[place, kk] = value

            legendre(place, core, put_b)

    def group_pair(n):
        to_core(n).wait_recv()
        for dz in (2, 1, 3, 0):
            kk = lax.rem(z + dz, 4)
            for place in range(*groups[n]):
                asend[place, dz] = (alm_b[place, kk] + pair[place, kk].astype(F32)).astype(BF16)
                if dz + place > 0:
                    to_owner(dz, place).start()

    for n in range(len(groups)):
        group_terms(n)
    for n in range(len(groups)):
        group_pair(n)
    arecv[e] = asend[0, 0]
    copied(arecv.at[pl.ds(0, 63)], ar_sem).wait_recv()
    loads[9].wait()
    parts = sum(arecv[16 * dz : 16 * dz + 16].astype(F32) for dz in range(4))
    alm = jnp.concatenate(
        [parts[:, 8 * gl : 8 * gl + 8, :].reshape(128, 128) for gl in range(3)], axis=1).astype(BF16)
    mixed = dot(ce[0], alm) + dot(ce[1], alm)
    scaled = (mixed * band[...]).astype(BF16)
    scaled = jnp.concatenate([scaled[:64], scaled[64:]], axis=1)
    sketch = jnp.concatenate([dot_nt(tt[h], scaled) for h in range(2)], axis=1)
    ssend[...] = sketch.reshape(2, 64, 2, 128)

    to_sibling = pltpu.make_async_remote_copy(
        src_ref=ssend.at[1 - core], dst_ref=srecv, send_sem=ss_sem, recv_sem=sr_sem,
        device_id=(2 * z + 1 - core, e), device_id_type=MESH)
    to_sibling.start()
    to_sibling.wait_recv()
    fsend[...] = ssend[core] + srecv[...]

    def to_column(dz, a, b):
        column = lax.rem(z + dz, 4) * 16 + ahead(a, b)
        return pltpu.make_async_remote_copy(
            src_ref=fsend.at[column], dst_ref=frecv.at[16 * z + e],
            send_sem=fs_sem, recv_sem=fr_sem,
            device_id=(plane(dz), ahead(a, b)), device_id_type=MESH)

    for dz, a, b in peers:
        to_column(dz, a, b).start()
    frecv[16 * z + e] = fsend[16 * z + e]
    copied(frecv.at[pl.ds(0, 63)], fr_sem).wait_recv()
    out[...] = jnp.sum(frecv[...], axis=0)

    copied(xrecv.at[:, pl.ds(0, NM - 1)], xs_sem).wait_send()
    copied(lall.at[pl.ds(0, 6)], ls_sem).wait_send()
    copied(lall.at[pl.ds(0, 9)], lf_sem).wait_send()
    copied(alm_a, ps_sem).wait_send()
    copied(arecv.at[pl.ds(0, 63)], as_sem).wait_send()
    to_sibling.wait_send()
    copied(frecv.at[pl.ds(0, 63)], fs_sem).wait_send()


def local(sky_map, pixel_mask, noise_factor, cycle_legendre, band_power, channel_cov, test_matrix):
    wa, wb, twc, tws = fourier_tables()
    args = (
        jnp.transpose(sky_map, (0, 2, 1)).reshape(512, 512),
        pixel_mask,
        noise_factor.reshape(512, 64),
        jnp.transpose(cycle_legendre, (0, 2, 1)).reshape(64, 384),
        jnp.transpose(band_power),
        channel_cov,
        test_matrix.reshape(384, 2, 512),
        wa, wb, twc, tws,
    )
    dma = pltpu.SemaphoreType.DMA
    result = pl.pallas_call(
        kernel,
        out_shape=jax.ShapeDtypeStruct((2, 128), F32),
        in_specs=[pl.BlockSpec(memory_space=pl.ANY)] * len(args),
        out_specs=pl.BlockSpec(memory_space=pltpu.VMEM),
        scratch_shapes=[
            pltpu.VMEM((512, 512), BF16),
            pltpu.VMEM((8, 512), jnp.int32),
            pltpu.VMEM((512, 64), F32),
            pltpu.VMEM((64, 384), F32),
            pltpu.VMEM((1, 384), F32),
            pltpu.VMEM((64, 64), F32),
            pltpu.VMEM((384, 2, 512), BF16),
            pltpu.VMEM((128, 64), BF16),
            pltpu.VMEM((96, 256), BF16),
            pltpu.VMEM((128, 128), F32),
            pltpu.VMEM((128, 128), F32),
            pltpu.VMEM((512, 512), BF16),
            pltpu.VMEM((2, 16, 16, 512), BF16),
            pltpu.VMEM((2, 16, 16, 512), BF16),
            pltpu.VMEM((2048, 128), F32),
            pltpu.VMEM((1024, 512), F32),
            pltpu.VMEM((16, 256, 256), BF16),
            pltpu.VMEM((2, 3, 32, 128), BF16),
            pltpu.VMEM((16, 2, 3, 32, 128), BF16),
            pltpu.VMEM((3072, 128), F32),
            pltpu.VMEM((3072, 128), F32),
            pltpu.VMEM((16, 4, 24, 128), BF16),
            pltpu.VMEM((16, 4, 24, 128), F32),
            pltpu.VMEM((16, 4, 24, 128), BF16),
            pltpu.VMEM((16, 4, 24, 128), BF16),
            pltpu.VMEM((64, 24, 128), BF16),
            pltpu.VMEM((2, 256, 768), BF16),
            pltpu.VMEM((2, 128, 128), BF16),
            pltpu.VMEM((2, 64, 2, 128), F32),
            pltpu.VMEM((64, 2, 128), F32),
            pltpu.VMEM((64, 2, 128), F32),
            pltpu.VMEM((64, 2, 128), F32),
            dma((11,)), dma, dma((2,)), dma, dma((2,)), dma, dma((3,)),
            dma, dma((5,)), dma, dma, dma, dma, dma, dma,
        ],
        compiler_params=pltpu.CompilerParams(collective_id=0, has_side_effects=True),
        name="harmonic_sketch",
    )(*args)
    return jnp.transpose(result.reshape(4, 64))


def solution(mesh):
    return jax.shard_map(
        local,
        mesh=mesh,
        in_specs=(
            P("patch", "mode", None),
            P("patch", "mode"),
            P("patch", "mode", None, None),
            P("patch", "mode", None),
            P("mode", "patch"),
            P(),
            P("patch", "mode", None, None),
        ),
        out_specs=P(None, ("patch", "mode")),
        check_vma=False,
    )
```

```python
import functools
import math

import jax
import jax.numpy as jnp
import numpy as np
from jax import lax
from jax.experimental import pallas as pl
from jax.experimental.pallas import tpu as pltpu
from jax.sharding import PartitionSpec as P

F32 = jnp.float32
BF16 = jnp.bfloat16
MESH = pl.DeviceIdType.MESH
NM = 16


def fourier_tables():
    m1 = np.arange(64)[:, None]
    j1 = np.arange(64)[None, :]
    angle = 2.0 * math.pi * ((m1 * j1) % 64) / 64.0
    wa = np.concatenate([np.cos(angle), -np.sin(angle)], axis=0)
    low = np.arange(128)[:, None]
    j2 = np.arange(128)[None, :]
    turn = 2.0 * math.pi * (low * j2) / 8192.0
    g = np.arange(48)[:, None]
    phi = 2.0 * math.pi * ((g * j2) % 64) / 64.0
    wb = np.zeros((48, 2, 2, 128))
    wb[:, 0, 0, :] = np.cos(phi)
    wb[:, 0, 1, :] = np.sin(phi)
    wb[:, 1, 0, :] = -np.sin(phi)
    wb[:, 1, 1, :] = np.cos(phi)
    return (
        jnp.asarray(wa.astype(np.float32), BF16),
        jnp.asarray(wb.reshape(96, 256).astype(np.float32), BF16),
        jnp.asarray(np.cos(turn), F32),
        jnp.asarray(np.sin(turn), F32),
    )


def iota2(shape, axis):
    return lax.broadcasted_iota(jnp.int32, shape, axis)


def onehot(test):
    return jnp.where(test, 1.0, 0.0).astype(BF16)


def dot(a, b):
    return jnp.dot(a, b, preferred_element_type=F32)


def dot_nt(a, b):
    return lax.dot_general(a, b, (((1,), (1,)), ((), ())), preferred_element_type=F32)


def kernel(
    sky_h, mask_h, noise_h, leg_h, band_h, cov_h, test_h, wa_h, wb_h, twc_h, tws_h,
    out,
    sky, mask, noise, leg, band, cov, test, wa, wb, twc, tws,
    bd, xsend, xrecv, xs, fa, turned, lown, lall, lf, four, alm_a, alm_b, pair, asend, arecv, tt, ce,
    ssend, srecv, fsend, frecv,
    in_sem, xs_sem, xr_sem, ls_sem, ld_sem, lf_sem, lr_sem, ps_sem, pr_sem,
    as_sem, ar_sem, ss_sem, sr_sem, fs_sem, fr_sem,
):
    p = lax.axis_index("patch")
    e = lax.axis_index("mode")
    core = lax.rem(p, 2)
    z = p // 2
    ex = e // 4
    ey = lax.rem(e, 4)

    def ahead(a, b):
        return lax.rem(ex + a, 4) * 4 + lax.rem(ey + b, 4)

    def behind(a, b):
        return lax.rem(ex + 4 - a, 4) * 4 + lax.rem(ey + 4 - b, 4)

    def plane(dz):
        return 2 * lax.rem(z + dz, 4) + core

    peers = [(dz, a, b) for dz in range(4) for a in range(4) for b in range(4) if dz + a + b > 0]
    peers.sort(key=lambda t: -sum(min(v, 4 - v) for v in t))

    barrier = pltpu.get_barrier_semaphore()
    pl.semaphore_signal(barrier, inc=1, device_id=(2 * z + 1 - core, e), device_id_type=MESH)
    greeted = [(dz, a, b) for dz, a, b in peers if dz == 0 or a + b == 0]
    for dz, a, b in greeted:
        pl.semaphore_signal(barrier, inc=1, device_id=(plane(dz), ahead(a, b)), device_id_type=MESH)

    hbm = (noise_h, sky_h, mask_h, leg_h, wa_h, twc_h, tws_h, wb_h, cov_h, band_h, test_h)
    vmem = (noise, sky, mask, leg, wa, twc, tws, wb, cov, band, test)
    loads = [pltpu.make_async_copy(a, b, in_sem.at[i]) for i, (a, b) in enumerate(zip(hbm, vmem))]
    for load in loads:
        load.start()

    row = iota2((512, 512), 0)
    lane = iota2((512, 512), 1)
    source = ((row >> 2) & 7) * 64 + (row >> 5) * 4 + (row & 3)
    order = onehot(lane == source)
    repeat = onehot((iota2((64, 512), 1) & 63) == iota2((64, 512), 0))
    loads[0].wait()
    moved = dot(order, noise[...].astype(BF16)).astype(BF16)
    wide = dot(moved, repeat)
    bd[...] = jnp.where((lane >> 6) == ((row >> 2) & 7), wide, 0.0).astype(BF16)
    loads[1].wait()
    loads[2].wait()
    for r in range(8):
        seen = jnp.broadcast_to(mask[r : r + 1, :].astype(F32), (64, 512)).astype(BF16)
        sky[64 * r : 64 * r + 64, :] = sky[64 * r : 64 * r + 64, :] * seen

    loads[3].wait()
    for h in range(2):
        for t in range(3):
            lown[h, t] = leg[32 * h : 32 * h + 32, 128 * t : 128 * t + 128].astype(BF16)

    def send_x(a, b, half):
        to = ahead(a, b)
        return pltpu.make_async_remote_copy(
            src_ref=xsend.at[half, to], dst_ref=xrecv.at[half, e], send_sem=xs_sem, recv_sem=xr_sem.at[half],
            device_id=(p, to), device_id_type=MESH)

    def send_l(a, b):
        return pltpu.make_async_remote_copy(
            src_ref=lown, dst_ref=lall.at[4 * a + b], send_sem=ls_sem, recv_sem=ld_sem.at[0 if a == 0 else 1],
            device_id=(p, ahead(a, b)), device_id_type=MESH)

    def relay_l(a, b, h):
        source, to = ((4 * a, ahead(0, b)), (b, ahead(a, 0)))[h]
        return pltpu.make_async_remote_copy(
            src_ref=lall.at[source, h], dst_ref=lall.at[4 * a + b, h],
            send_sem=lf_sem, recv_sem=lr_sem.at[a],
            device_id=(p, to), device_id_type=MESH)

    straight = [(0, 2), (2, 0), (0, 1), (0, 3), (1, 0), (3, 0)]

    pl.semaphore_wait(barrier, len(greeted) + 1)
    for a, b in straight:
        send_l(a, b).start()
    for n in range(4):
        q = lax.rem(ex + n, 4)
        white = dot(bd[pl.ds(pl.multiple_of(128 * q, 128), 128), :], sky[...]).astype(BF16)
        white = white.reshape(4, 32, 512)
        for half in range(2):
            xsend[half, pl.ds(4 * q, 4)] = white[:, 16 * half : 16 * half + 16, :]
        for b in range(4):
            if n + b > 0:
                send_x(n, b, 0).start()
    for a in range(4):
        for b in range(4):
            if a + b > 0:
                send_x(a, b, 1).start()

    loads[10].wait()
    loads[8].wait()
    split = onehot(iota2((256, 256), 1) == 2 * (iota2((256, 256), 0) & 127) + (iota2((256, 256), 0) >> 7))
    to = iota2((256, 512), 0)
    wanted = ((to >> 5) & 3) * 128 + (to >> 7) * 64 + ((to >> 1) & 15) * 4 + (to & 1) * 2
    columns = [onehot(iota2((256, 512), 1) == wanted + h) for h in range(2)]
    for b in range(3):
        block = dot(split, test[128 * b : 128 * b + 128].reshape(256, 512)).astype(BF16)
        for h in range(2):
            parts = dot_nt(columns[h], block).astype(BF16)
            tt[h, :, 128 * b : 128 * b + 128] = parts[:, :128]
            tt[h, :, 384 + 128 * b : 384 + 128 * b + 128] = parts[:, 128:]
    l128 = iota2((64, 128), 1)
    spread = onehot(iota2((64, 128), 0) == 4 * (l128 >> 3) + (l128 & 3))
    high = cov[...].astype(BF16)
    rest = (cov[...] - high.astype(F32)).astype(BF16)
    for n, piece in enumerate((high, rest)):
        wide_cov = dot(piece, spread)
        for t in range(2):
            ce[n, 64 * t : 64 * t + 64, :] = jnp.where(((l128 >> 2) & 1) == t, wide_cov, 0.0).astype(BF16)

    def copied(ref, sem):
        return pltpu.make_async_remote_copy(
            src_ref=ref, dst_ref=ref, send_sem=sem, recv_sem=sem, device_id=(p, e), device_id_type=MESH)

    def spread_x(ref, half, src):
        for h in range(4):
            xs[pl.ds(1024 * half + src * 4 + h, 16, stride=64), :] = (
                ref[half, src, :, 128 * h : 128 * h + 128].astype(F32))

    def spread_l(ref, slot):
        for h in range(2):
            for t in range(3):
                lf[192 * slot + 64 * t + 32 * h : 192 * slot + 64 * t + 32 * h + 32, :] = ref[h, t].astype(F32)

    spread_x(xsend, 0, e)
    spread_x(xsend, 1, e)
    spread_l(lown, 0)
    copied(lall.at[pl.ds(0, 3)], ld_sem.at[1]).wait_recv()
    for n in (1, 3, 2):
        for b in (2, 1, 3):
            relay_l(n, b, 0).start()
    copied(lall.at[pl.ds(0, 3)], ld_sem.at[0]).wait_recv()
    for n in (1, 3, 2):
        for a in (2, 1, 3):
            relay_l(a, n, 1).start()
    for a, b in straight:
        spread_l(lall.at[4 * a + b], 4 * a + b)
    for n in (4, 5, 6, 7):
        loads[n].wait()

    def twiddle(r, carry):
        for h in range(2):
            c = twc[64 * h : 64 * h + 64, :]
            sn = tws[64 * h : 64 * h + 64, :]
            rows = pl.ds(pl.multiple_of(lax.rem(r, 2) * 128 + 64 * h, 64), 64)
            for dd in range(4):
                cols = slice(128 * dd, 128 * dd + 128)
                re = fa[pl.ds(pl.multiple_of(128 * r, 128), 64), cols]
                im = fa[pl.ds(pl.multiple_of(128 * r + 64, 64), 64), cols]
                unit = 4 * (r // 2) + dd
                turned[unit, rows, 0:128] = (re * c + im * sn).astype(BF16)
                turned[unit, rows, 128:256] = (im * c - re * sn).astype(BF16)
        return carry

    for half in range(2):
        copied(xrecv.at[half, pl.ds(0, NM - 1)], xr_sem.at[half]).wait_recv()

        def take_x(i, carry, half=half):
            spread_x(xrecv, half, lax.rem(e + i, NM))
            return carry

        lax.fori_loop(1, NM, take_x, 0)
        for r in range(4 * half, 4 * half + 4):
            pix = jnp.concatenate([xs[256 * r + 64 * dd : 256 * r + 64 * dd + 64, :] for dd in range(4)], axis=1)
            fa[128 * r : 128 * r + 128, :] = dot(wa[...], pix.astype(BF16))
        lax.fori_loop(4 * half, 4 * half + 4, twiddle, 0)
        for unit in range(8 * half, 8 * half + 8):
            second = dot_nt(wb[...], turned[unit])
            for s in range(2):
                start = (2 * (unit // 4) + s) * 384 + unit % 4
                four[pl.ds(start, 96, stride=4), :] = second[:, 128 * s : 128 * s + 128]

    def legendre(a, parity, put):
        def body(j, carry):
            acc = [[None, None] for _ in range(4)]
            for gi in range(2):
                q = 2 * j + gi
                b = q // 3
                g = 3 * (lax.rem(ex + 4 - a, 4) * 4 + lax.rem(ey + 4 - b, 4)) + q - 3 * b
                for r in range(8):
                    f = four[pl.ds(pl.multiple_of(r * 384 + g * 8, 8), 8), :]
                    for kk in range(4):
                        lrow = lf[pl.ds((12 * a + q) * 64 + r * 8 + 2 * kk + parity, 8, stride=0), :]
                        term = lrow * f
                        acc[kk][gi] = term if r == 0 else acc[kk][gi] + term
            for kk in range(4):
                put(kk, pl.ds(pl.multiple_of(j * 16, 16), 16), jnp.concatenate(acc[kk], axis=0))
            return carry

        lax.fori_loop(0, 6, body, 0, unroll=3)

    def to_core(n):
        return pltpu.make_async_remote_copy(
            src_ref=alm_a.at[n], dst_ref=pair.at[n], send_sem=ps_sem, recv_sem=pr_sem.at[n],
            device_id=(2 * z + 1 - core, e), device_id_type=MESH)

    def to_owner(dz, n, b):
        return pltpu.make_async_remote_copy(
            src_ref=asend.at[n, dz, b], dst_ref=arecv.at[16 * dz + e],
            send_sem=as_sem, recv_sem=ar_sem,
            device_id=(plane(dz), behind(n, b)), device_id_type=MESH)

    def group_terms(n):
        if n > 0:
            copied(lall.at[pl.ds(0, 3)], lr_sem.at[n]).wait_recv()
            for b in range(1, 4):
                spread_l(lall.at[4 * n + b], 4 * n + b)

        def put_a(kk, rows, value):
            alm_a[n, kk, rows, :] = value.astype(BF16)

        def put_b(kk, rows, value):
            alm_b[n, kk, rows, :] = value

        legendre(n, 1 - core, put_a)
        to_core(n).start()
        legendre(n, core, put_b)

    def group_pair(n):
        to_core(n).wait_recv()
        for dz in (2, 1, 3, 0):
            kk = lax.rem(z + dz, 4)
            both = (alm_b[n, kk] + pair[n, kk].astype(F32)).astype(BF16)
            for b in (2, 1, 3, 0):
                asend[n, dz, b] = both[24 * b : 24 * b + 24, :]
                if dz + n + b > 0:
                    to_owner(dz, n, b).start()

    for n in range(4):
        group_terms(n)
    for n in range(4):
        group_pair(n)
    arecv[e] = asend[0, 0, 0]
    copied(arecv.at[pl.ds(0, 63)], ar_sem).wait_recv()
    loads[9].wait()
    parts = sum(arecv[16 * dz : 16 * dz + 16].astype(F32) for dz in range(4))
    alm = jnp.concatenate(
        [parts[:, 8 * gl : 8 * gl + 8, :].reshape(128, 128) for gl in range(3)], axis=1).astype(BF16)
    mixed = dot(ce[0], alm) + dot(ce[1], alm)
    scaled = (mixed * band[...]).astype(BF16)
    scaled = jnp.concatenate([scaled[:64], scaled[64:]], axis=1)
    sketch = jnp.concatenate([dot_nt(tt[h], scaled) for h in range(2)], axis=1)
    ssend[...] = sketch.reshape(2, 64, 2, 128)

    to_sibling = pltpu.make_async_remote_copy(
        src_ref=ssend.at[1 - core], dst_ref=srecv, send_sem=ss_sem, recv_sem=sr_sem,
        device_id=(2 * z + 1 - core, e), device_id_type=MESH)
    to_sibling.start()
    to_sibling.wait_recv()
    fsend[...] = ssend[core] + srecv[...]

    def to_column(dz, a, b):
        column = lax.rem(z + dz, 4) * 16 + ahead(a, b)
        return pltpu.make_async_remote_copy(
            src_ref=fsend.at[column], dst_ref=frecv.at[16 * z + e],
            send_sem=fs_sem, recv_sem=fr_sem,
            device_id=(plane(dz), ahead(a, b)), device_id_type=MESH)

    for dz, a, b in peers:
        to_column(dz, a, b).start()
    frecv[16 * z + e] = fsend[16 * z + e]
    copied(frecv.at[pl.ds(0, 63)], fr_sem).wait_recv()
    out[...] = jnp.sum(frecv[...], axis=0)

    copied(xrecv.at[:, pl.ds(0, NM - 1)], xs_sem).wait_send()
    copied(lall.at[pl.ds(0, 6)], ls_sem).wait_send()
    copied(lall.at[pl.ds(0, 9)], lf_sem).wait_send()
    copied(alm_a, ps_sem).wait_send()
    copied(arecv.at[pl.ds(0, 63)], as_sem).wait_send()
    to_sibling.wait_send()
    copied(frecv.at[pl.ds(0, 63)], fs_sem).wait_send()


def local(sky_map, pixel_mask, noise_factor, cycle_legendre, band_power, channel_cov, test_matrix):
    wa, wb, twc, tws = fourier_tables()
    args = (
        jnp.transpose(sky_map, (0, 2, 1)).reshape(512, 512),
        pixel_mask,
        noise_factor.reshape(512, 64),
        jnp.transpose(cycle_legendre, (0, 2, 1)).reshape(64, 384),
        jnp.transpose(band_power),
        channel_cov,
        test_matrix.reshape(384, 2, 512),
        wa, wb, twc, tws,
    )
    dma = pltpu.SemaphoreType.DMA
    result = pl.pallas_call(
        kernel,
        out_shape=jax.ShapeDtypeStruct((2, 128), F32),
        in_specs=[pl.BlockSpec(memory_space=pl.ANY)] * len(args),
        out_specs=pl.BlockSpec(memory_space=pltpu.VMEM),
        scratch_shapes=[
            pltpu.VMEM((512, 512), BF16),
            pltpu.VMEM((8, 512), jnp.int32),
            pltpu.VMEM((512, 64), F32),
            pltpu.VMEM((64, 384), F32),
            pltpu.VMEM((1, 384), F32),
            pltpu.VMEM((64, 64), F32),
            pltpu.VMEM((384, 2, 512), BF16),
            pltpu.VMEM((128, 64), BF16),
            pltpu.VMEM((96, 256), BF16),
            pltpu.VMEM((128, 128), F32),
            pltpu.VMEM((128, 128), F32),
            pltpu.VMEM((512, 512), BF16),
            pltpu.VMEM((2, 16, 16, 512), BF16),
            pltpu.VMEM((2, 16, 16, 512), BF16),
            pltpu.VMEM((2112, 128), F32),
            pltpu.VMEM((1024, 512), F32),
            pltpu.VMEM((16, 256, 256), BF16),
            pltpu.VMEM((2, 3, 32, 128), BF16),
            pltpu.VMEM((16, 2, 3, 32, 128), BF16),
            pltpu.VMEM((3080, 128), F32),
            pltpu.VMEM((3080, 128), F32),
            pltpu.VMEM((4, 4, 96, 128), BF16),
            pltpu.VMEM((4, 4, 96, 128), F32),
            pltpu.VMEM((4, 4, 96, 128), BF16),
            pltpu.VMEM((4, 4, 4, 24, 128), BF16),
            pltpu.VMEM((64, 24, 128), BF16),
            pltpu.VMEM((2, 256, 768), BF16),
            pltpu.VMEM((2, 128, 128), BF16),
            pltpu.VMEM((2, 64, 2, 128), F32),
            pltpu.VMEM((64, 2, 128), F32),
            pltpu.VMEM((64, 2, 128), F32),
            pltpu.VMEM((64, 2, 128), F32),
            dma((11,)), dma, dma((2,)), dma, dma((2,)), dma, dma((4,)),
            dma, dma((4,)), dma, dma, dma, dma, dma, dma,
        ],
        compiler_params=pltpu.CompilerParams(collective_id=0, has_side_effects=True),
        name="harmonic_sketch",
    )(*args)
    return jnp.transpose(result.reshape(4, 64))


def solution(mesh):
    return jax.shard_map(
        local,
        mesh=mesh,
        in_specs=(
            P("patch", "mode", None),
            P("patch", "mode"),
            P("patch", "mode", None, None),
            P("patch", "mode", None),
            P("mode", "patch"),
            P(),
            P("patch", "mode", None, None),
        ),
        out_specs=P(None, ("patch", "mode")),
        check_vma=False,
    )
```
